32 devices in a mesh: groups: 2 (over y), ctx: 8 (over z, core), chan: 2 (over x).
Axes of the slice: x: 2, y: 2, z: 4, core: 2. Of those that a mesh axis runs over, the one named last changes fastest.
Arguments:
- tokens: bfloat16 [4096, 2048], P(('groups', 'ctx')), parts along dimension 0, may hold values from -6 to 6
- in_weight: bfloat16 [2048, 3, 2048], P('ctx', None, 'chan'), may hold values from -0.125 to 0.125
- short_taps: bfloat16 [3, 3, 2048], P(None, None, 'chan'), may hold values from -3.5 to 3.5
- filters: bfloat16 [2048, 2048], P('chan', 'ctx'), may hold values from -0.125 to 0.125
- doc_lengths: int32 [8], P('groups'), parts along dimension 0, may hold values from 1 to 1024, 2048 in all
- out_weight: bfloat16 [2048, 2048], P('chan', 'ctx'), may hold values from -0.125 to 0.125
Outputs:
- output: bfloat16 [4096, 2048], P(('groups', 'ctx', 'chan')), parts along dimension 0
The draws below stay inside these ranges and needn't reach their ends.
There are 2 independent parts, one for each index of `groups`. The reference program is written for one: setup_inputs(seed, part) draws one part's arguments, and reference() takes and returns one part's arrays. A program takes and returns all parts, laid end to end along the dimension named above; an argument that names none is the same for every part. Nothing has to cross between parts.
Inputs may be any that keep to these rules, and one draw needn't show every extreme that they name: doc_lengths are the lengths of the solutions packed one after another; they fill all 2048 positions.
All inputs are finite; a program needn't handle non-finite values.
Results may differ from the reference program's by a relative error of at most 0.007.
Values may be sent and summed in bfloat16 or wider, within the bound.
A program may use at most 64 MiB of HBM per device.

```python
import math
import jax
import jax.numpy as jnp
import numpy as np
from jax import lax

D = 2048
CH = 2048
SEQ = 2048
NDOCS = 4
MOST_LEN = 1024


def block_levels(own_key, shape, pieces, least, high):
    def one(dim, parts):
        heights = jax.random.uniform(jax.random.fold_in(jax.random.fold_in(own_key, 6), dim), (parts,), jnp.float32, least / len(pieces), high / len(pieces))
        return jnp.repeat(jnp.exp(heights), shape[dim] // parts).reshape((-1,) + (1,) * (len(shape) - dim - 1))

    gain = one(*pieces[0])
    for cut in pieces[1:]:
        gain = gain * one(*cut)
    return gain


def split_up(amount, total, most, lean):
    weights = [(1 << 20) // math.isqrt(grade ** lean) + 1 for grade in range(2, amount + 1)]
    rest, given = total - most - (amount - 1), [1] * (amount - 1)
    while rest > 0:
        free = [i for i in range(amount - 1) if given[i] < most]
        whole, budget = sum([weights[i] for i in free]), rest
        for i in free:
            addition = min(most - given[i], max(1, budget * weights[i] // whole), rest)
            given[i] = given[i] + addition
            rest = rest - addition
    return np.array([most] + given)


def ragged(rng, number_of, total, bound, slope):
    if number_of == 2:
        one = jax.random.randint(rng, (), max(1, total - bound), min(bound, total - 1) + 1)
        return jnp.stack([one, total - one])
    sizes = jnp.asarray(split_up(number_of, total, bound, slope), jnp.int32)
    pairs = (number_of - 1) // 2
    donor, receiver = sizes[1:1 + 2 * pairs:2], sizes[2:2 + 2 * pairs:2]
    margin = jnp.minimum(donor - 1, bound - receiver)
    passed = jax.random.randint(jax.random.fold_in(rng, 1), (pairs,), 0, 1 << 20) % (margin + 1)
    sizes = sizes.at[1:1 + 2 * pairs:2].set(donor - passed).at[2:2 + 2 * pairs:2].set(receiver + passed)
    return sizes[jax.random.permutation(jax.random.fold_in(rng, 2), number_of)]


def noise(rng, dims, scale, reach, split=(), kind=jnp.bfloat16):
    values = jax.random.normal(rng, dims, jnp.float32) * scale
    if len(split) > 0:
        values = block_levels(rng, dims, split, -0.22, 0.18) * values
    return jnp.clip(values, min=-reach, max=reach).astype(kind)


def setup_inputs(seed: int = 0, part: int = 0) -> dict:
    splits = jax.random.split(jax.random.key(seed), 7)
    own_keys = jax.random.split(jax.random.fold_in(splits[6], part), 7)
    return {
        "tokens": noise(own_keys[0], (SEQ, D), 1.0, 6.0, ((0, 8),)),
        "in_weight": noise(splits[1], (D, 3, CH), D ** -0.5, 0.125, ((0, 8), (2, 2))),
        "short_taps": noise(splits[2], (3, 3, CH), 3 ** -0.5, 3.5, ((2, 2),)),
        "filters": noise(splits[3], (CH, SEQ), SEQ ** -0.5, 0.125, ((0, 2), (1, 8))),
        "doc_lengths": ragged(own_keys[4], NDOCS, SEQ, MOST_LEN, 1).astype(jnp.int32),
        "out_weight": noise(splits[5], (CH, D), CH ** -0.5, 0.125, ((0, 2), (1, 8))),
    }


def document_ids(doc_lengths, seq_len):
    ends = jnp.cumsum(doc_lengths, dtype=jnp.int32)
    places = lax.broadcasted_iota(jnp.int32, (seq_len, ends.shape[0]), 0)
    return jnp.sum((places >= ends[None, :]).astype(jnp.int32), axis=1)


def short_conv(streams, taps, doc_id):
    result = taps[:, 0, :, None] * streams
    for lag in (1, 2):
        moved = jnp.pad(streams, ((0, 0), (0, 0), (lag, 0)))[:, :, :-lag]
        linked = jnp.concatenate((jnp.zeros((lag,), bool), doc_id[lag:] == doc_id[:-lag]))
        result = result + taps[:, lag, :, None] * jnp.where(linked[None, None, :], moved, 0.0)
    return result


def long_filter(gated, kernel):
    seq_len = gated.shape[-1]
    spectrum = jnp.fft.rfft(gated, n=2 * seq_len) * jnp.fft.rfft(kernel, n=2 * seq_len)
    return jnp.fft.irfft(spectrum, n=2 * seq_len)[..., :seq_len].astype(gated.dtype)


def reference(tokens, in_weight, short_taps, filters, doc_lengths, out_weight):
    seq_len = tokens.shape[0]
    doc_id = document_ids(doc_lengths, seq_len)
    block = math.gcd(CH, 256)
    tokens_wide = tokens.astype(jnp.float32)

    def one_block(index):
        offset = (index * block).astype(jnp.int32)
        weight = lax.dynamic_slice_in_dim(in_weight, offset, block, 2).astype(jnp.float32)
        streams = jnp.einsum("td,dsc->sct", tokens_wide, weight).astype(jnp.bfloat16)
        streams = lax.optimization_barrier(streams).astype(jnp.float32)
        taps = lax.dynamic_slice_in_dim(short_taps, offset, block, 2).astype(jnp.float32)
        conv = short_conv(streams, taps, doc_id)
        kernel = lax.dynamic_slice_in_dim(filters, offset, block, 0).astype(jnp.float32)
        filtered = long_filter(conv[0] * conv[2], kernel)
        return (conv[1] * filtered).astype(jnp.bfloat16)

    mixed = lax.map(one_block, jnp.arange(CH // block, dtype=jnp.int32)).reshape(CH, seq_len)
    output = lax.dot_general(mixed, out_weight, (((0,), (0,)), ((), ())), preferred_element_type=jnp.float32)
    return output.astype(jnp.bfloat16)
```

```python
import functools
import math

import jax
import jax.numpy as jnp
from jax import lax
from jax.experimental import pallas as pl
from jax.experimental.pallas import tpu as pltpu
from jax.sharding import PartitionSpec as P

def contract(form, left, right):
    return jnp.einsum(form, left, right, precision=lax.Precision.HIGHEST)


def angle_table(rows, cols, period):
    product = lax.broadcasted_iota(jnp.int32, (rows, cols), 0) * lax.broadcasted_iota(
        jnp.int32, (rows, cols), 1
    )
    theta = (product % period).astype(jnp.float32) * (2.0 * math.pi / period)
    return (jnp.cos(theta), jnp.sin(theta))


def document_ids(doc_lengths, seq_len):
    count = doc_lengths.shape[0]
    order = lax.broadcasted_iota(jnp.int32, (count, count), 0)
    before = order >= lax.broadcasted_iota(jnp.int32, (count, count), 1)
    ends = jnp.sum(jnp.where(before, doc_lengths[None, :], 0), axis=1)
    places = lax.broadcasted_iota(jnp.int32, (seq_len, ends.shape[0]), 0)
    return jnp.sum((places >= ends[None, :]).astype(jnp.int32), axis=1)


def short_conv(streams, taps, doc_id):
    result = taps[:, 0, :, None] * streams
    for lag in (1, 2):
        moved = jnp.pad(streams, ((0, 0), (0, 0), (lag, 0)))[:, :, :-lag]
        linked = jnp.concatenate((jnp.zeros((lag,), bool), doc_id[lag:] == doc_id[:-lag]))
        result = result + taps[:, lag, :, None] * jnp.where(linked[None, None, :], moved, 0.0)
    return result


def causal_filter(gated, kernel_rows):
    count, seq_len = gated.shape
    width = math.gcd(seq_len, 128)
    half = seq_len // width
    span = 2 * half
    total = span * width
    signal = gated.reshape(count, half, width)
    kernel = kernel_rows.reshape(count, half, width)
    cos_b, sin_b = angle_table(span, span, span)
    twist_c, twist_s = angle_table(span, width, total)
    cos_a, sin_a = angle_table(width, width, width)

    def forward(values):
        padded = jnp.concatenate((values, jnp.zeros_like(values)), 1)
        real_part = contract("kb,cba->cka", cos_b, padded)
        imag_part = -contract("kb,cba->cka", sin_b, padded)
        turned_r = real_part * twist_c + imag_part * twist_s
        turned_i = imag_part * twist_c - real_part * twist_s
        spec_r = contract("cka,aj->ckj", turned_r, cos_a) + contract("cka,aj->ckj", turned_i, sin_a)
        spec_i = contract("cka,aj->ckj", turned_i, cos_a) - contract("cka,aj->ckj", turned_r, sin_a)
        return (spec_r, spec_i)

    sig_r, sig_i = forward(signal)
    ker_r, ker_i = forward(kernel)
    prod_r = sig_r * ker_r - sig_i * ker_i
    prod_i = sig_r * ker_i + sig_i * ker_r
    back_r = contract("ckj,aj->cka", prod_r, cos_a) - contract("ckj,aj->cka", prod_i, sin_a)
    back_i = contract("ckj,aj->cka", prod_i, cos_a) + contract("ckj,aj->cka", prod_r, sin_a)
    untwist_r = back_r * twist_c - back_i * twist_s
    untwist_i = back_i * twist_c + back_r * twist_s
    blocks = contract("bk,cka->cba", cos_b, untwist_r) - contract("bk,cka->cba", sin_b, untwist_i)
    blocks = blocks[:, :half]
    return (blocks / total).reshape(count, seq_len)


def shards(tokens, in_weight, short_taps, filters, doc_lengths, out_weight):
    width_dev = in_weight.shape[2]
    group_width = width_dev // lax.axis_size("ctx")
    streams = jnp.einsum(
        "dsc,td->sct",
        lax.all_gather(in_weight, "ctx", axis=0, tiled=True),
        tokens,
        preferred_element_type=jnp.float32,
    )
    packed = jnp.concatenate((streams.astype(jnp.bfloat16), filters[None]), 0)
    spread = lax.all_to_all(packed, "ctx", split_axis=1, concat_axis=2, tiled=True)
    taps = lax.dynamic_slice_in_dim(
        short_taps, lax.axis_index("ctx") * group_width, group_width, 2
    ).astype(jnp.float32)
    seq_len = spread.shape[2]
    doc_id = document_ids(doc_lengths, seq_len)
    conv = short_conv(spread[:3].astype(jnp.float32), taps, doc_id)
    filtered = causal_filter(conv[0] * conv[2], spread[3].astype(jnp.float32))
    mixed = (conv[1] * filtered).astype(jnp.bfloat16)
    returned = lax.all_to_all(mixed, "ctx", split_axis=1, concat_axis=0, tiled=True)
    partial_out = lax.dot_general(
        returned,
        lax.all_gather(out_weight, "ctx", axis=1, tiled=True),
        (((0,), (0,)), ((), ())),
        preferred_element_type=jnp.float32,
    )
    return lax.psum_scatter(partial_out, "chan", scatter_dimension=0, tiled=True).astype(
        jnp.bfloat16
    )


TILE = 128
HALF = 64
THICK = 16
MESH = pl.DeviceIdType.MESH


def spread_taps(taps_ref, taps, chans, me):
    for s in range(3):
        rows = taps_ref[s, :, pl.ds(pl.multiple_of(me * chans, TILE), chans)].astype(jnp.float32)
        for lag in range(3):
            taps[3 * s + lag] = jnp.broadcast_to(rows[lag : lag + 1, :], (TILE, chans)).T


def mark_links(docs_ref, keep, blocks):
    lane = lax.broadcasted_iota(jnp.int32, (8, TILE), 1)
    ends = []
    for j in range(docs_ref.shape[0]):
        ends.append(docs_ref[j] + ends[-1] if j else docs_ref[j])
    for b in range(blocks):
        place = lane + b * TILE
        for lag in (1, 2):
            linked = place >= lag
            for end in ends:
                linked = jnp.logical_and(
                    linked, jnp.logical_or(place < end, place - lag >= end)
                )
            keep[lag - 1, b] = linked.astype(jnp.float32)


def build_band(index, kernels, bands):
    seq = kernels.shape[1]
    lane = lax.broadcasted_iota(jnp.int32, (THICK, TILE), 1)
    place = lane % HALF - lax.broadcasted_iota(jnp.int32, (THICK, TILE), 0)
    low = lane < HALF
    for pair in range(2):
        rows = [
            jnp.broadcast_to(kernels[pl.ds(4 * index + 2 * pair + u, 1), :], (THICK, seq))
            for u in range(2)
        ]
        for q in range(TILE // THICK):
            moved = [
                pltpu.roll(
                    rows[u],
                    (seq - HALF * (1 - u) + q * THICK) % seq,
                    1,
                    stride=1,
                    stride_axis=0,
                )
                for u in range(2)
            ]
            for m in range(seq // TILE):
                span = slice(m * TILE, (m + 1) * TILE)
                tile = jnp.where(low, moved[0][:, span], moved[1][:, span])
                if m == 0:
                    tile = jnp.where(place + HALF >= q * THICK, tile, 0.0)
                first = (m % 2) * TILE + q * THICK
                bands[
                    index, m // 2, first : first + THICK, pair * TILE : (pair + 1) * TILE
                ] = tile.astype(jnp.bfloat16)


def filter_group(index, streams, taps, keep, bands, mixed, chans):
    blocks = keep.shape[1]
    lane = lax.broadcasted_iota(jnp.int32, (8, TILE), 1)
    sub = lax.broadcasted_iota(jnp.int32, (8, TILE), 0)
    left, top = lane < HALF, sub < 4
    second = (sub & 2) > 0
    straight = ((sub & 1) == 0) != top
    products = []
    for half in range(2):
        first = pl.multiple_of(index * 16 + 8 * half, 8)
        rows = pl.ds(first, 8)
        conv = [None] * 3
        for s in range(3):
            tap = [taps[3 * s + lag, rows, :] for lag in range(3)]
            conv[s] = []
            before = [None, None]
            for b in range(blocks):
                value = streams[s, b, rows, :]
                total = tap[0] * value
                for lag in (1, 2):
                    rolled = pltpu.roll(value, lag, 1)
                    moved = rolled
                    if b:
                        moved = jnp.where(lane < lag, before[lag - 1], rolled)
                    before[lag - 1] = rolled
                    total = total + tap[lag] * (keep[lag - 1, b] * moved)
                conv[s].append(total)
        gated = [conv[0][b] * conv[2][b] for b in range(blocks)]
        turned = [pltpu.roll(gated[b], HALF, 1) for b in range(blocks)]
        late = [
            jnp.where(left, turned[b - 1] if b else 0.0, turned[b]) for b in range(blocks)
        ]
        packed = []
        for quad in range(2):
            if quad == 0:
                rows_of = [
                    jnp.where(top, gated[b], pltpu.roll(late[b], 4, 0)) for b in range(blocks)
                ]
            else:
                rows_of = [
                    jnp.where(top, pltpu.roll(gated[b], 4, 0), late[b]) for b in range(blocks)
                ]
            now = jnp.concatenate(rows_of, axis=0).astype(jnp.bfloat16)
            old = jnp.concatenate(
                [jnp.zeros_like(rows_of[0])] + rows_of[:-1], axis=0
            ).astype(jnp.bfloat16)
            packed.append(jnp.concatenate([now, old], axis=1))
        straights, swapped = [], []
        for quad in range(2):
            which = 4 * index + 2 * half + quad
            sums = [None] * blocks
            for t in range(blocks // 2):
                height = 8 * blocks - 16 * t
                part = jnp.dot(
                    packed[quad][:height], bands[which, t], preferred_element_type=jnp.float32
                )
                for b in range(2 * t, blocks):
                    piece = part[8 * (b - 2 * t) : 8 * (b - 2 * t) + 8]
                    sums[b] = piece if sums[b] is None else sums[b] + piece
            one, two = [], []
            for b in range(blocks):
                both = jnp.where(second, sums[b][:, TILE:], sums[b][:, :TILE])
                both = jnp.where(straight, both, pltpu.roll(both, HALF, 1))
                one.append(both)
                two.append(pltpu.roll(both, 4, 0))
            straights.append(one)
            swapped.append(two)
        result = []
        for b in range(blocks):
            upper = jnp.where(left, swapped[0][b], straights[0][b])
            lower = jnp.where(left, straights[1][b], swapped[1][b])
            result.append(conv[1][b] * jnp.where(top, upper, lower))
        products.append(result)
    for b in range(blocks):
        mixed[b, pl.ds(pl.multiple_of(index * 16, 16), 16), :] = jnp.concatenate(
            [products[0][b], products[1][b]], axis=0
        ).astype(jnp.bfloat16)


def exchange_kernel(
    planes,
    cuts,
    parts,
    weight_ref,
    filters_ref,
    tokens_ref,
    outw_ref,
    taps_ref,
    docs_ref,
    out_ref,
    toks,
    raw,
    wide,
    lags,
    outw,
    streams,
    kernels,
    bands,
    mixed,
    arrived,
    turned,
    taps,
    keep,
    local_sem,
    own_send,
    own_recv,
    tok_z_send,
    tok_z_recv,
    tok_x_send,
    tok_x_recv,
    tok_c_send,
    tok_c_recv,
    w_send,
    w_recv,
    w_y_send,
    w_y_recv,
    f_send,
    f_recv,
    f_y_send,
    f_y_recv,
    o_z_send,
    o_z_recv,
    o_x_send,
    o_x_recv,
    o_y_send,
    o_y_recv,
    o_c_send,
    o_c_recv,
    m_send,
    m_recv,
):
    g = lax.axis_index("groups")
    k = lax.axis_index("ctx")
    x = lax.axis_index("chan")
    z, core = k // 2, k % 2
    count = 2 * planes
    blocks = 2 * count
    rows = tokens_ref.shape[0]
    lanes = rows // 2
    piece = lanes // cuts
    depth = weight_ref.shape[1]
    half_d = depth // 2
    half_o = outw_ref.shape[0] // 2
    chans = kernels.shape[0]
    other = 2 * z + 1 - core

    def at(group=g, ctx=k, chan=x):
        return (group, ctx, chan)

    def remote(src, dst, send, recv, where):
        return pltpu.make_async_remote_copy(
            src_ref=src,
            dst_ref=dst,
            send_sem=send,
            recv_sem=recv,
            device_id=where,
            device_id_type=MESH,
        )

    def tile_of(index):
        return pl.ds(pl.multiple_of(index * TILE, TILE), TILE)

    def when(condition, action):
        pl.when(condition)(action)

    peers = []
    for far in range(2):
        for step in range(count):
            if far or step:
                peers.append((far, step))

    def peer(far, step):
        return ((k + step) % count, 1 - x if far else x)

    barrier = pltpu.get_barrier_semaphore()
    for far, step in peers:
        to, side = peer(far, step)
        pl.semaphore_signal(
            barrier, inc=1, device_id=at(ctx=to, chan=side), device_id_type=MESH
        )
    pl.semaphore_signal(barrier, inc=1, device_id=at(group=1 - g), device_id_type=MESH)
    pl.semaphore_wait(barrier, len(peers) + 1)

    def lag_column(owner, half):
        return lags.at[:, tile_of(2 * owner + half)]

    def lags_of(owner, half):
        return filters_ref.at[tile_of(owner), tile_of(half)]

    def weight_rows(owner, half):
        return raw.at[:, pl.ds(pl.multiple_of(owner * depth + half * half_d, TILE), half_d), :]

    def weight_of(owner, half):
        return weight_ref.at[:, pl.ds(pl.multiple_of(half * half_d, TILE), half_d), tile_of(owner)]

    def tok(owner, half, cut):
        return toks.at[owner, pl.ds(pl.multiple_of(half * lanes + cut * piece, piece), piece), :]

    def outw_at(side, owner, half):
        return outw.at[side, owner, pl.ds(pl.multiple_of(half * half_o, half_o), half_o), :]

    flights = []

    def launch(copy):
        copy.start()
        flights.append(copy)
        return copy

    f_copies = [
        launch(
            remote(
                lags_of((k + step) % count, g),
                lag_column(k, g),
                f_send.at[step],
                f_recv.at[step],
                at(ctx=(k + step) % count),
            )
        )
        for step in range(1, count)
    ]

    locals_ = [
        pltpu.make_async_copy(lags_of(k, 0), lag_column(k, 0), local_sem.at[0]),
        pltpu.make_async_copy(lags_of(k, 1), lag_column(k, 1), local_sem.at[1]),
        pltpu.make_async_copy(weight_of(k, 0), weight_rows(k, 0), local_sem.at[2]),
        pltpu.make_async_copy(weight_of(k, 1), weight_rows(k, 1), local_sem.at[3]),
        pltpu.make_async_copy(tokens_ref, toks.at[k], local_sem.at[4]),
        pltpu.make_async_copy(outw_ref, outw.at[x, k], local_sem.at[5]),
    ]
    for copy in locals_[:2]:
        copy.start()

    guarded = []

    def present(side, step):
        return z >= step if side == 0 else z + step < planes

    def onward(side):
        return z + 1 < planes if side == 0 else z >= 1

    def origin(side, step):
        return 2 * (z - step if side == 0 else z + step) + core

    def beyond(side):
        return at(ctx=2 * (z + 1 if side == 0 else z - 1) + core)

    def hop(side, step, make):
        ready = onward(side)
        if step > 1:
            ready = jnp.logical_and(ready, present(side, step - 1))

        def go():
            make().start()

        when(ready, go)
        guarded.append((ready, make))

    def tok_hop(side, step, cut):
        def make():
            if step == 1:
                source = tokens_ref.at[
                    pl.ds(pl.multiple_of(x * lanes + cut * piece, piece), piece), :
                ]
            else:
                source = tok(origin(side, step - 1), x, cut)
            return remote(
                source,
                tok(origin(side, step - 1), x, cut),
                tok_z_send.at[side, step, cut],
                tok_z_recv.at[side, step, cut],
                beyond(side),
            )

        hop(side, step, make)

    for cut in range(cuts):
        for side in range(2):
            tok_hop(side, 1, cut)

    w_copies = [
        launch(
            remote(
                weight_of((k + step) % count, g),
                weight_rows(k, g),
                w_send.at[step],
                w_recv.at[step],
                at(ctx=(k + step) % count),
            )
        )
        for step in range(1, count)
    ]
    for copy in locals_[2:]:
        copy.start()
    core_own = launch(
        remote(tokens_ref, toks.at[k], own_send.at[0], own_recv.at[0], at(ctx=other))
    )
    core_own_o = launch(
        remote(outw_ref, outw.at[x, k], own_send.at[1], own_recv.at[1], at(ctx=other))
    )
    side_own_o = launch(
        remote(outw_ref, outw.at[x, k], own_send.at[2], own_recv.at[2], at(chan=1 - x))
    )

    spread_taps(taps_ref, taps, chans, k)
    mark_links(docs_ref, keep, blocks)

    fy_copies = []
    for step in range(1, count):
        f_copies[step - 1].wait_recv()
        came = lag_column((k + count - step) % count, g)
        fy_copies.append(
            launch(remote(came, came, f_y_send.at[step], f_y_recv.at[step], at(group=1 - g)))
        )
    for copy in fy_copies:
        copy.wait_recv()
    for copy in locals_[:2]:
        copy.wait()
    kernels[...] = lags[...].astype(jnp.float32)

    total = bands.shape[0]
    done = [0]

    def work(amount):
        first, last = done[0], min(done[0] + amount, total)
        done[0] = last

        def body(index, carry):
            build_band(index, kernels, bands)
            return carry

        if last > first:
            lax.fori_loop(first, last, body, 0)

    def tok_z(side, step, cut):
        came = tok(origin(side, step), x, cut)
        return remote(
            came, came, tok_z_send.at[side, step, cut], tok_z_recv.at[side, step, cut], at(ctx=other)
        )

    def tok_x(side, step, half, cut):
        came = tok(origin(side, step), half, cut)
        return remote(
            came, came, tok_x_send.at[side, step, cut], tok_x_recv.at[side, step, cut], at(chan=1 - x)
        )

    def tok_c(side, step, half, which, cut):
        came = tok(origin(side, step), half, cut)
        return remote(
            came,
            came,
            tok_c_send.at[which, side, step, cut],
            tok_c_recv.at[which, side, step, cut],
            at(ctx=other),
        )

    def tok_relay(step, cut):
        for side in range(2):

            def arrive(side=side):
                tok_z(side, step, cut).wait_recv()

            when(present(side, step), arrive)
            if step + 1 < planes:
                tok_hop(side, step + 1, cut)

            def share(side=side):
                tok_x(side, step, x, cut).start()
                tok_c(side, step, x, 0, cut).start()

            when(present(side, step), share)

    def tok_cross(step, cut):
        for side in range(2):

            def arrive(side=side):
                tok_x(side, step, 1 - x, cut).wait_recv()
                tok_c(side, step, 1 - x, 1, cut).start()

            when(present(side, step), arrive)

    def project(index, carry):
        value = lax.dot_general(
            wide[...],
            toks[index],
            (((1,), (1,)), ((), ())),
            preferred_element_type=jnp.float32,
        )
        value = value.astype(jnp.bfloat16).astype(jnp.float32)
        for s in range(3):
            for h in range(2):
                streams[s, 2 * index + h] = value[
                    s * chans : (s + 1) * chans, h * TILE : (h + 1) * TILE
                ]
        return carry

    def tok_done(step):
        for side in range(2):

            def arrive(side=side):
                for cut in range(cuts):
                    for which in range(2):
                        tok_c(side, step, which, which, cut).wait_recv()

                def both(index, carry):
                    return project(2 * (origin(side, step) // 2) + index, carry)

                lax.fori_loop(0, 2, both, 0)

            when(present(side, step), arrive)

    def outw_hop(side, step):
        def make():
            if step == 1:
                source = outw_ref.at[pl.ds(pl.multiple_of(g * half_o, half_o), half_o), :]
            else:
                source = outw_at(x, origin(side, step - 1), g)
            return remote(
                source,
                outw_at(x, origin(side, step - 1), g),
                o_z_send.at[side, step],
                o_z_recv.at[side, step],
                beyond(side),
            )

        hop(side, step, make)

    def outw_move(kind, side, step, near, half):
        came = outw_at(x if near else 1 - x, origin(side, step), half)
        if kind == "z":
            return remote(
                came, came, o_z_send.at[side, step], o_z_recv.at[side, step], at(ctx=other)
            )
        if kind == "x":
            return remote(
                came, came, o_x_send.at[side, step], o_x_recv.at[side, step], at(chan=1 - x)
            )
        if kind == "y":
            which = 0 if near else 1
            return remote(
                came,
                came,
                o_y_send.at[which, side, step],
                o_y_recv.at[which, side, step],
                at(group=1 - g),
            )
        which = int(kind)
        return remote(
            came,
            came,
            o_c_send.at[which, side, step],
            o_c_recv.at[which, side, step],
            at(ctx=other),
        )

    def outw_relay(step):
        for side in range(2):

            def arrive(side=side):
                outw_move("z", side, step, True, g).wait_recv()

            when(present(side, step), arrive)
            if step + 1 < planes:
                outw_hop(side, step + 1)

            def share(side=side):
                outw_move("x", side, step, True, g).start()
                outw_move("y", side, step, True, g).start()
                outw_move("0", side, step, True, g).start()

            when(present(side, step), share)

    def outw_cross(step):
        for side in range(2):

            def arrive(side=side):
                outw_move("x", side, step, False, g).wait_recv()
                outw_move("y", side, step, False, g).start()
                outw_move("1", side, step, False, g).start()

            when(present(side, step), arrive)

    def outw_last(step):
        for side in range(2):

            def arrive(side=side):
                outw_move("y", side, step, True, 1 - g).wait_recv()
                outw_move("2", side, step, True, 1 - g).start()
                outw_move("y", side, step, False, 1 - g).wait_recv()
                outw_move("3", side, step, False, 1 - g).start()

            when(present(side, step), arrive)

    def outw_done(step):
        for side in range(2):

            def arrive(side=side):
                outw_move("0", side, step, True, g).wait_recv()
                outw_move("1", side, step, False, g).wait_recv()
                outw_move("2", side, step, True, 1 - g).wait_recv()
                outw_move("3", side, step, False, 1 - g).wait_recv()

            when(present(side, step), arrive)

    quota = total // (2 * planes)
    for cut in range(cuts):
        tok_relay(1, cut)
        work(quota // 2)
    wy_copies = []
    for step in range(1, count):
        w_copies[step - 1].wait_recv()
        came = weight_rows((k + count - step) % count, g)
        wy_copies.append(
            launch(remote(came, came, w_y_send.at[step], w_y_recv.at[step], at(group=1 - g)))
        )
        work(1)
    for step in range(2, planes):
        for cut in range(cuts):
            if step == planes - 1:
                break
            tok_relay(step, cut)
            tok_cross(step - 1, cut)
            work(quota // 2 + 1)
    work(total)
    side_own_o.wait_recv()
    came_o = outw.at[1 - x, k]
    core_own_x = launch(
        remote(came_o, came_o, own_send.at[3], own_recv.at[3], at(ctx=other))
    )
    for copy in locals_[2:]:
        copy.wait()
    for copy in wy_copies:
        copy.wait_recv()

    def stand(index, carry):
        place = pl.ds(pl.multiple_of(index * TILE, TILE), TILE)
        for s in range(3):
            wide[s * chans : (s + 1) * chans, place] = (
                raw[s, place, :].astype(jnp.float32).T.astype(jnp.bfloat16)
            )
        return carry

    lax.fori_loop(0, raw.shape[1] // TILE, stand, 0)
    core_own.wait_recv()
    last = planes - 1
    for cut in range(cuts):
        tok_relay(last, cut)
        if last > 1:
            tok_cross(last - 1, cut)
        if cut == 0:
            project(k, 0)
            project(other, 0)
        elif cut == 1:
            for step in range(1, last - 1):
                tok_done(step)
    for side in range(2):
        outw_hop(side, 1)
    tok_done(last - 1)
    for cut in range(cuts):
        tok_cross(last, cut)
    tok_done(last)

    groups = chans // 16 // parts

    def filter_step(index, carry):
        filter_group(index, streams, taps, keep, bands, mixed, chans)
        return carry

    for part in range(parts):
        lax.fori_loop(part * groups, (part + 1) * groups, filter_step, 0)
        span = pl.ds(part * groups * 16, groups * 16)
        for far, step in peers:
            to, side = peer(far, step)
            launch(
                remote(
                    mixed.at[2 * to + side, span, :],
                    arrived.at[x * count + k, span, :],
                    m_send.at[part, far, step],
                    m_recv.at[part, far, step],
                    at(ctx=to, chan=side),
                )
            )
        if part + 1 < planes:
            outw_relay(part + 1)
            if part:
                outw_cross(part)
    for step in range(parts + 1, planes):
        outw_relay(step)
    for step in range(max(1, min(parts, planes - 1)), planes):
        outw_cross(step)
    own_mixed = pltpu.make_async_copy(
        mixed.at[2 * k + x], arrived.at[x * count + k], local_sem.at[0]
    )
    own_mixed.start()
    own_mixed.wait()
    for part in range(parts):
        for far, step in peers:
            came = arrived.at[x * count + k, pl.ds(part * groups * 16, groups * 16), :]
            remote(
                came, came, m_send.at[part, far, step], m_recv.at[part, far, step], at(ctx=other)
            ).wait_recv()
    for owner in range(2 * count):
        turned[:, owner * chans : (owner + 1) * chans] = (
            arrived[owner].astype(jnp.float32).T.astype(jnp.bfloat16)
        )
    for step in range(1, planes):
        outw_last(step)
    core_own_o.wait_recv()
    core_own_x.wait_recv()
    for step in range(1, planes):
        outw_done(step)

    wide_e = outw_ref.shape[1]
    near = count * chans
    for owner in range(count):
        out_ref[:, owner * wide_e : (owner + 1) * wide_e] = (
            jnp.dot(turned[:, :near], outw[0, owner], preferred_element_type=jnp.float32)
            + jnp.dot(turned[:, near:], outw[1, owner], preferred_element_type=jnp.float32)
        ).astype(jnp.bfloat16)

    for copy in flights:
        copy.wait_send()
    for ready, make in guarded:

        def left(make=make):
            make().wait_send()

        when(ready, left)
    for step in range(1, planes):
        for side in range(2):

            def gone(side=side, step=step):
                for cut in range(cuts):
                    tok_x(side, step, x, cut).wait_send()
                    tok_c(side, step, x, 0, cut).wait_send()
                    tok_c(side, step, 1 - x, 1, cut).wait_send()
                outw_move("x", side, step, True, g).wait_send()
                outw_move("y", side, step, True, g).wait_send()
                outw_move("y", side, step, False, g).wait_send()
                outw_move("0", side, step, True, g).wait_send()
                outw_move("1", side, step, False, g).wait_send()
                outw_move("2", side, step, True, 1 - g).wait_send()
                outw_move("3", side, step, False, 1 - g).wait_send()

            when(present(side, step), gone)


CUTS = 4
PARTS = 4


def fused(tokens, in_weight, short_taps, filters, doc_lengths, out_weight):
    count = lax.axis_size("ctx")
    chans = in_weight.shape[2] // count
    rows, model = tokens.shape
    seq_len = filters.shape[1] * count
    blocks = seq_len // TILE
    planes = count // 2
    dma = pltpu.SemaphoreType.DMA
    anywhere = pl.BlockSpec(memory_space=pl.ANY)
    vmem = pl.BlockSpec(memory_space=pltpu.VMEM)
    return pl.pallas_call(
        functools.partial(exchange_kernel, planes, CUTS, PARTS),
        out_shape=jax.ShapeDtypeStruct((rows // 2, model), jnp.bfloat16),
        in_specs=[anywhere] * 4 + [vmem, pl.BlockSpec(memory_space=pltpu.SMEM)],
        out_specs=vmem,
        scratch_shapes=[
            pltpu.VMEM((count, rows, model), jnp.bfloat16),
            pltpu.VMEM((3, model, chans), jnp.bfloat16),
            pltpu.VMEM((3 * chans, model), jnp.bfloat16),
            pltpu.VMEM((chans, seq_len), jnp.bfloat16),
            pltpu.VMEM((2, count) + out_weight.shape, jnp.bfloat16),
            pltpu.VMEM((3, blocks, chans, TILE), jnp.float32),
            pltpu.VMEM((chans, seq_len), jnp.float32),
            pltpu.VMEM((chans // 4, blocks // 2, 2 * TILE, 2 * TILE), jnp.bfloat16),
            pltpu.VMEM((blocks, chans, TILE), jnp.bfloat16),
            pltpu.VMEM((2 * count, chans, TILE), jnp.bfloat16),
            pltpu.VMEM((TILE, 2 * count * chans), jnp.bfloat16),
            pltpu.VMEM((9, chans, TILE), jnp.float32),
            pltpu.VMEM((2, blocks, 8, TILE), jnp.float32),
            dma((6,)),
            dma((4,)),
            dma((4,)),
        ]
        + [dma((2, planes, CUTS))] * 4
        + [dma((2, 2, planes, CUTS))] * 2
        + [dma((count,))] * 8
        + [dma((2, planes))] * 4
        + [dma((2, 2, planes))] * 2
        + [dma((4, 2, planes))] * 2
        + [dma((PARTS, 2, count))] * 2,
        compiler_params=pltpu.CompilerParams(
            collective_id=0, has_side_effects=True, vmem_limit_bytes=61 * 1024 * 1024
        ),
    )(in_weight.transpose(1, 0, 2), filters, tokens, out_weight, short_taps, doc_lengths)


def fits(tokens, in_weight, filters, out_weight):
    count = lax.axis_size("ctx")
    rows, model = tokens.shape
    return (
        count % 2 == 0
        and count >= 6
        and lax.axis_size("chan") == 2
        and lax.axis_size("groups") == 2
        and in_weight.shape[0] == 2 * TILE
        and in_weight.shape[2] == count * TILE
        and filters.shape[1] == 2 * TILE
        and rows == 2 * TILE
        and out_weight.shape[1] == 2 * TILE
        and model == 2 * TILE * count
        and count * rows * model * 2 <= 8 * 1024 * 1024
    )


def layer(tokens, in_weight, short_taps, filters, doc_lengths, out_weight):
    if fits(tokens, in_weight, filters, out_weight):
        return fused(tokens, in_weight, short_taps, filters, doc_lengths, out_weight)
    return shards(tokens, in_weight, short_taps, filters, doc_lengths, out_weight)


def solution(mesh):
    placed = (
        P(("groups", "ctx"), None),
        P("ctx", None, "chan"),
        P(None, None, "chan"),
        P("chan", "ctx"),
        P("groups"),
        P("chan", "ctx"),
    )
    return jax.shard_map(
        layer,
        mesh=mesh,
        in_specs=placed,
        out_specs=P(("groups", "ctx", "chan"), None),
        check_vma=False,
    )
```

```python
import functools
import math

import jax
import jax.numpy as jnp
from jax import lax
from jax.experimental import pallas as pl
from jax.experimental.pallas import tpu as pltpu
from jax.sharding import PartitionSpec as P

def contract(form, left, right):
    return jnp.einsum(form, left, right, precision=lax.Precision.HIGHEST)


def angle_table(rows, cols, period):
    product = lax.broadcasted_iota(jnp.int32, (rows, cols), 0) * lax.broadcasted_iota(
        jnp.int32, (rows, cols), 1
    )
    theta = (product % period).astype(jnp.float32) * (2.0 * math.pi / period)
    return (jnp.cos(theta), jnp.sin(theta))


def document_ids(doc_lengths, seq_len):
    count = doc_lengths.shape[0]
    order = lax.broadcasted_iota(jnp.int32, (count, count), 0)
    before = order >= lax.broadcasted_iota(jnp.int32, (count, count), 1)
    ends = jnp.sum(jnp.where(before, doc_lengths[None, :], 0), axis=1)
    places = lax.broadcasted_iota(jnp.int32, (seq_len, ends.shape[0]), 0)
    return jnp.sum((places >= ends[None, :]).astype(jnp.int32), axis=1)


def short_conv(streams, taps, doc_id):
    result = taps[:, 0, :, None] * streams
    for lag in (1, 2):
        moved = jnp.pad(streams, ((0, 0), (0, 0), (lag, 0)))[:, :, :-lag]
        linked = jnp.concatenate((jnp.zeros((lag,), bool), doc_id[lag:] == doc_id[:-lag]))
        result = result + taps[:, lag, :, None] * jnp.where(linked[None, None, :], moved, 0.0)
    return result


def causal_filter(gated, kernel_rows):
    count, seq_len = gated.shape
    width = math.gcd(seq_len, 128)
    half = seq_len // width
    span = 2 * half
    total = span * width
    signal = gated.reshape(count, half, width)
    kernel = kernel_rows.reshape(count, half, width)
    cos_b, sin_b = angle_table(span, span, span)
    twist_c, twist_s = angle_table(span, width, total)
    cos_a, sin_a = angle_table(width, width, width)

    def forward(values):
        padded = jnp.concatenate((values, jnp.zeros_like(values)), 1)
        real_part = contract("kb,cba->cka", cos_b, padded)
        imag_part = -contract("kb,cba->cka", sin_b, padded)
        turned_r = real_part * twist_c + imag_part * twist_s
        turned_i = imag_part * twist_c - real_part * twist_s
        spec_r = contract("cka,aj->ckj", turned_r, cos_a) + contract("cka,aj->ckj", turned_i, sin_a)
        spec_i = contract("cka,aj->ckj", turned_i, cos_a) - contract("cka,aj->ckj", turned_r, sin_a)
        return (spec_r, spec_i)

    sig_r, sig_i = forward(signal)
    ker_r, ker_i = forward(kernel)
    prod_r = sig_r * ker_r - sig_i * ker_i
    prod_i = sig_r * ker_i + sig_i * ker_r
    back_r = contract("ckj,aj->cka", prod_r, cos_a) - contract("ckj,aj->cka", prod_i, sin_a)
    back_i = contract("ckj,aj->cka", prod_i, cos_a) + contract("ckj,aj->cka", prod_r, sin_a)
    untwist_r = back_r * twist_c - back_i * twist_s
    untwist_i = back_i * twist_c + back_r * twist_s
    blocks = contract("bk,cka->cba", cos_b, untwist_r) - contract("bk,cka->cba", sin_b, untwist_i)
    blocks = blocks[:, :half]
    return (blocks / total).reshape(count, seq_len)


def shards(tokens, in_weight, short_taps, filters, doc_lengths, out_weight):
    width_dev = in_weight.shape[2]
    group_width = width_dev // lax.axis_size("ctx")
    streams = jnp.einsum(
        "dsc,td->sct",
        lax.all_gather(in_weight, "ctx", axis=0, tiled=True),
        tokens,
        preferred_element_type=jnp.float32,
    )
    packed = jnp.concatenate((streams.astype(jnp.bfloat16), filters[None]), 0)
    spread = lax.all_to_all(packed, "ctx", split_axis=1, concat_axis=2, tiled=True)
    taps = lax.dynamic_slice_in_dim(
        short_taps, lax.axis_index("ctx") * group_width, group_width, 2
    ).astype(jnp.float32)
    seq_len = spread.shape[2]
    doc_id = document_ids(doc_lengths, seq_len)
    conv = short_conv(spread[:3].astype(jnp.float32), taps, doc_id)
    filtered = causal_filter(conv[0] * conv[2], spread[3].astype(jnp.float32))
    mixed = (conv[1] * filtered).astype(jnp.bfloat16)
    returned = lax.all_to_all(mixed, "ctx", split_axis=1, concat_axis=0, tiled=True)
    partial_out = lax.dot_general(
        returned,
        lax.all_gather(out_weight, "ctx", axis=1, tiled=True),
        (((0,), (0,)), ((), ())),
        preferred_element_type=jnp.float32,
    )
    return lax.psum_scatter(partial_out, "chan", scatter_dimension=0, tiled=True).astype(
        jnp.bfloat16
    )


TILE = 128
HALF = 64
THICK = 16
MESH = pl.DeviceIdType.MESH


def spread_taps(taps_ref, taps, chans, me):
    for s in range(3):
        rows = taps_ref[s, :, pl.ds(pl.multiple_of(me * chans, TILE), chans)].astype(jnp.float32)
        for lag in range(3):
            taps[3 * s + lag] = jnp.broadcast_to(rows[lag : lag + 1, :], (TILE, chans)).T


def mark_links(docs_ref, keep, blocks):
    lane = lax.broadcasted_iota(jnp.int32, (8, TILE), 1)
    ends = []
    for j in range(docs_ref.shape[0]):
        ends.append(docs_ref[j] + ends[-1] if j else docs_ref[j])
    for b in range(blocks):
        place = lane + b * TILE
        for lag in (1, 2):
            linked = place >= lag
            for end in ends:
                linked = jnp.logical_and(
                    linked, jnp.logical_or(place < end, place - lag >= end)
                )
            keep[lag - 1, b] = linked.astype(jnp.float32)


def build_band(index, kernels, bands):
    seq = kernels.shape[1]
    lane = lax.broadcasted_iota(jnp.int32, (THICK, TILE), 1)
    place = lane % HALF - lax.broadcasted_iota(jnp.int32, (THICK, TILE), 0)
    low = lane < HALF
    for pair in range(2):
        rows = [
            jnp.broadcast_to(kernels[pl.ds(4 * index + 2 * pair + u, 1), :], (THICK, seq))
            for u in range(2)
        ]
        for q in range(TILE // THICK):
            moved = [
                pltpu.roll(
                    rows[u],
                    (seq - HALF * (1 - u) + q * THICK) % seq,
                    1,
                    stride=1,
                    stride_axis=0,
                )
                for u in range(2)
            ]
            for m in range(seq // TILE):
                span = slice(m * TILE, (m + 1) * TILE)
                tile = jnp.where(low, moved[0][:, span], moved[1][:, span])
                if m == 0:
                    tile = jnp.where(place + HALF >= q * THICK, tile, 0.0)
                first = (m % 2) * TILE + q * THICK
                bands[
                    index, m // 2, first : first + THICK, pair * TILE : (pair + 1) * TILE
                ] = tile.astype(jnp.bfloat16)


def filter_group(index, streams, taps, keep, bands, mixed, chans):
    blocks = keep.shape[1]
    lane = lax.broadcasted_iota(jnp.int32, (8, TILE), 1)
    sub = lax.broadcasted_iota(jnp.int32, (8, TILE), 0)
    left, top = lane < HALF, sub < 4
    second = (sub & 2) > 0
    straight = ((sub & 1) == 0) != top
    products = []
    for half in range(2):
        first = pl.multiple_of(index * 16 + 8 * half, 8)
        rows = pl.ds(first, 8)
        conv = [None] * 3
        for s in range(3):
            tap = [taps[3 * s + lag, rows, :] for lag in range(3)]
            conv[s] = []
            before = [None, None]
            for b in range(blocks):
                value = streams[s, b, rows, :]
                total = tap[0] * value
                for lag in (1, 2):
                    rolled = pltpu.roll(value, lag, 1)
                    moved = rolled
                    if b:
                        moved = jnp.where(lane < lag, before[lag - 1], rolled)
                    before[lag - 1] = rolled
                    total = total + tap[lag] * (keep[lag - 1, b] * moved)
                conv[s].append(total)
        gated = [conv[0][b] * conv[2][b] for b in range(blocks)]
        turned = [pltpu.roll(gated[b], HALF, 1) for b in range(blocks)]
        late = [
            jnp.where(left, turned[b - 1] if b else 0.0, turned[b]) for b in range(blocks)
        ]
        packed = []
        for quad in range(2):
            if quad == 0:
                rows_of = [
                    jnp.where(top, gated[b], pltpu.roll(late[b], 4, 0)) for b in range(blocks)
                ]
            else:
                rows_of = [
                    jnp.where(top, pltpu.roll(gated[b], 4, 0), late[b]) for b in range(blocks)
                ]
            now = jnp.concatenate(rows_of, axis=0).astype(jnp.bfloat16)
            old = jnp.concatenate(
                [jnp.zeros_like(rows_of[0])] + rows_of[:-1], axis=0
            ).astype(jnp.bfloat16)
            packed.append(jnp.concatenate([now, old], axis=1))
        straights, swapped = [], []
        for quad in range(2):
            which = 4 * index + 2 * half + quad
            sums = [None] * blocks
            for t in range(blocks // 2):
                height = 8 * blocks - 16 * t
                part = jnp.dot(
                    packed[quad][:height], bands[which, t], preferred_element_type=jnp.float32
                )
                for b in range(2 * t, blocks):
                    piece = part[8 * (b - 2 * t) : 8 * (b - 2 * t) + 8]
                    sums[b] = piece if sums[b] is None else sums[b] + piece
            one, two = [], []
            for b in range(blocks):
                both = jnp.where(second, sums[b][:, TILE:], sums[b][:, :TILE])
                both = jnp.where(straight, both, pltpu.roll(both, HALF, 1))
                one.append(both)
                two.append(pltpu.roll(both, 4, 0))
            straights.append(one)
            swapped.append(two)
        result = []
        for b in range(blocks):
            upper = jnp.where(left, swapped[0][b], straights[0][b])
            lower = jnp.where(left, straights[1][b], swapped[1][b])
            result.append(conv[1][b] * jnp.where(top, upper, lower))
        products.append(result)
    for b in range(blocks):
        mixed[b, pl.ds(pl.multiple_of(index * 16, 16), 16), :] = jnp.concatenate(
            [products[0][b], products[1][b]], axis=0
        ).astype(jnp.bfloat16)


def exchange_kernel(
    planes,
    cuts,
    parts,
    weight_ref,
    filters_ref,
    tokens_ref,
    outw_ref,
    taps_ref,
    docs_ref,
    out_ref,
    toks,
    raw,
    wide,
    lags,
    outw,
    streams,
    kernels,
    bands,
    mixed,
    arrived,
    turned,
    own_part,
    sent_part,
    got_part,
    taps,
    keep,
    local_sem,
    own_send,
    own_recv,
    tok_z_send,
    tok_z_recv,
    tok_x_send,
    tok_x_recv,
    tok_c_send,
    tok_c_recv,
    w_send,
    w_recv,
    w_y_send,
    w_y_recv,
    f_send,
    f_recv,
    f_y_send,
    f_y_recv,
    o_z_send,
    o_z_recv,
    o_y_send,
    o_y_recv,
    o_c_send,
    o_c_recv,
    m_send,
    m_recv,
    p_send,
    p_recv,
):
    g = lax.axis_index("groups")
    k = lax.axis_index("ctx")
    x = lax.axis_index("chan")
    z, core = k // 2, k % 2
    count = 2 * planes
    blocks = 2 * count
    rows = tokens_ref.shape[0]
    lanes = rows // 2
    piece = lanes // cuts
    depth = weight_ref.shape[1]
    half_d = depth // 2
    half_o = outw_ref.shape[0] // 2
    chans = kernels.shape[0]
    other = 2 * z + 1 - core

    def at(group=g, ctx=k, chan=x):
        return (group, ctx, chan)

    def remote(src, dst, send, recv, where):
        return pltpu.make_async_remote_copy(
            src_ref=src,
            dst_ref=dst,
            send_sem=send,
            recv_sem=recv,
            device_id=where,
            device_id_type=MESH,
        )

    def tile_of(index):
        return pl.ds(pl.multiple_of(index * TILE, TILE), TILE)

    def when(condition, action):
        pl.when(condition)(action)

    barrier = pltpu.get_barrier_semaphore()
    for step in range(1, count):
        pl.semaphore_signal(
            barrier, inc=1, device_id=at(ctx=(k + step) % count), device_id_type=MESH
        )
    pl.semaphore_signal(barrier, inc=1, device_id=at(chan=1 - x), device_id_type=MESH)
    pl.semaphore_signal(barrier, inc=1, device_id=at(group=1 - g), device_id_type=MESH)
    pl.semaphore_wait(barrier, count + 1)

    def lag_column(owner, half):
        return lags.at[:, tile_of(2 * owner + half)]

    def lags_of(owner, half):
        return filters_ref.at[tile_of(owner), tile_of(half)]

    def weight_rows(owner, half):
        return raw.at[:, pl.ds(pl.multiple_of(owner * depth + half * half_d, TILE), half_d), :]

    def weight_of(owner, half):
        return weight_ref.at[:, pl.ds(pl.multiple_of(half * half_d, TILE), half_d), tile_of(owner)]

    def tok(owner, half, cut):
        return toks.at[owner, pl.ds(pl.multiple_of(half * lanes + cut * piece, piece), piece), :]

    def outw_at(owner, half):
        return outw.at[owner, pl.ds(pl.multiple_of(half * half_o, half_o), half_o), :]

    flights = []

    def launch(copy):
        copy.start()
        flights.append(copy)
        return copy

    f_copies = [
        launch(
            remote(
                lags_of((k + step) % count, g),
                lag_column(k, g),
                f_send.at[step],
                f_recv.at[step],
                at(ctx=(k + step) % count),
            )
        )
        for step in range(1, count)
    ]

    locals_ = [
        pltpu.make_async_copy(lags_of(k, 0), lag_column(k, 0), local_sem.at[0]),
        pltpu.make_async_copy(lags_of(k, 1), lag_column(k, 1), local_sem.at[1]),
        pltpu.make_async_copy(weight_of(k, 0), weight_rows(k, 0), local_sem.at[2]),
        pltpu.make_async_copy(weight_of(k, 1), weight_rows(k, 1), local_sem.at[3]),
        pltpu.make_async_copy(tokens_ref, toks.at[k], local_sem.at[4]),
        pltpu.make_async_copy(outw_ref, outw.at[k], local_sem.at[5]),
    ]
    for copy in locals_[:2]:
        copy.start()

    guarded = []

    def present(side, step):
        return z >= step if side == 0 else z + step < planes

    def onward(side):
        return z + 1 < planes if side == 0 else z >= 1

    def origin(side, step):
        return 2 * (z - step if side == 0 else z + step) + core

    def beyond(side):
        return at(ctx=2 * (z + 1 if side == 0 else z - 1) + core)

    def hop(side, step, make, only=None):
        ready = onward(side)
        if only is not None:
            ready = jnp.logical_and(ready, only)
        if step > 1:
            ready = jnp.logical_and(ready, present(side, step - 1))

        def go():
            make().start()

        when(ready, go)
        guarded.append((ready, make))

    def tok_hop(side, step, cut):
        def make():
            if step == 1:
                source = tokens_ref.at[
                    pl.ds(pl.multiple_of(x * lanes + cut * piece, piece), piece), :
                ]
            else:
                source = tok(origin(side, step - 1), x, cut)
            return remote(
                source,
                tok(origin(side, step - 1), x, cut),
                tok_z_send.at[side, step, cut],
                tok_z_recv.at[side, step, cut],
                beyond(side),
            )

        hop(side, step, make)

    for cut in range(cuts):
        for side in range(2):
            tok_hop(side, 1, cut)

    w_copies = [
        launch(
            remote(
                weight_of((k + step) % count, g),
                weight_rows(k, g),
                w_send.at[step],
                w_recv.at[step],
                at(ctx=(k + step) % count),
            )
        )
        for step in range(1, count)
    ]
    for copy in locals_[2:]:
        copy.start()
    core_own = launch(
        remote(tokens_ref, toks.at[k], own_send.at[0], own_recv.at[0], at(ctx=other))
    )
    core_own_o = launch(
        remote(outw_ref, outw.at[k], own_send.at[1], own_recv.at[1], at(ctx=other))
    )

    spread_taps(taps_ref, taps, chans, k)
    mark_links(docs_ref, keep, blocks)

    fy_copies = []
    for step in range(1, count):
        f_copies[step - 1].wait_recv()
        came = lag_column((k + count - step) % count, g)
        fy_copies.append(
            launch(remote(came, came, f_y_send.at[step], f_y_recv.at[step], at(group=1 - g)))
        )
    for copy in fy_copies:
        copy.wait_recv()
    for copy in locals_[:2]:
        copy.wait()
    kernels[...] = lags[...].astype(jnp.float32)

    total = bands.shape[0]
    done = [0]

    def work(amount):
        first, last = done[0], min(done[0] + amount, total)
        done[0] = last

        def body(index, carry):
            build_band(index, kernels, bands)
            return carry

        if last > first:
            lax.fori_loop(first, last, body, 0)

    def tok_z(side, step, cut):
        came = tok(origin(side, step), x, cut)
        return remote(
            came, came, tok_z_send.at[side, step, cut], tok_z_recv.at[side, step, cut], at(ctx=other)
        )

    def tok_x(side, step, half, cut):
        came = tok(origin(side, step), half, cut)
        return remote(
            came, came, tok_x_send.at[side, step, cut], tok_x_recv.at[side, step, cut], at(chan=1 - x)
        )

    def tok_c(side, step, half, which, cut):
        came = tok(origin(side, step), half, cut)
        return remote(
            came,
            came,
            tok_c_send.at[which, side, step, cut],
            tok_c_recv.at[which, side, step, cut],
            at(ctx=other),
        )

    def tok_relay(step, cut):
        for side in range(2):

            def arrive(side=side):
                tok_z(side, step, cut).wait_recv()

            when(present(side, step), arrive)
            if step + 1 < planes:
                tok_hop(side, step + 1, cut)

            def share(side=side):
                tok_x(side, step, x, cut).start()
                tok_c(side, step, x, 0, cut).start()

            when(present(side, step), share)

    def tok_cross(step, cut):
        for side in range(2):

            def arrive(side=side):
                tok_x(side, step, 1 - x, cut).wait_recv()
                tok_c(side, step, 1 - x, 1, cut).start()

            when(present(side, step), arrive)

    def project(index, carry):
        value = lax.dot_general(
            wide[...],
            toks[index],
            (((1,), (1,)), ((), ())),
            preferred_element_type=jnp.float32,
        )
        value = value.astype(jnp.bfloat16).astype(jnp.float32)
        for s in range(3):
            for h in range(2):
                streams[s, 2 * index + h] = value[
                    s * chans : (s + 1) * chans, h * TILE : (h + 1) * TILE
                ]
        return carry

    def tok_done(step):
        for side in range(2):

            def arrive(side=side):
                for cut in range(cuts):
                    for which in range(2):
                        tok_c(side, step, which, which, cut).wait_recv()

                def both(index, carry):
                    return project(2 * (origin(side, step) // 2) + index, carry)

                lax.fori_loop(0, 2, both, 0)

            when(present(side, step), arrive)

    def outw_hop(side, step, only=None):
        def make():
            if step == 1:
                source = outw_ref.at[pl.ds(pl.multiple_of(g * half_o, half_o), half_o), :]
            else:
                source = outw_at(origin(side, step - 1), g)
            return remote(
                source,
                outw_at(origin(side, step - 1), g),
                o_z_send.at[side, step],
                o_z_recv.at[side, step],
                beyond(side),
            )

        hop(side, step, make, only)

    def outw_move(kind, side, step, half):
        came = outw_at(origin(side, step), half)
        if kind == "z":
            sems, where = (o_z_send.at[side, step], o_z_recv.at[side, step]), at(ctx=other)
        elif kind == "y":
            sems, where = (o_y_send.at[side, step], o_y_recv.at[side, step]), at(group=1 - g)
        else:
            which = int(kind)
            sems = (o_c_send.at[which, side, step], o_c_recv.at[which, side, step])
            where = at(ctx=other)
        return remote(came, came, sems[0], sems[1], where)

    def outw_relay(step):
        for side in range(2):

            def arrive(side=side):
                outw_move("z", side, step, g).wait_recv()

            when(present(side, step), arrive)
            if step + 1 < planes:
                outw_hop(side, step + 1)

            def share(side=side):
                outw_move("y", side, step, g).start()
                outw_move("0", side, step, g).start()

            when(present(side, step), share)

    def outw_last(step):
        for side in range(2):

            def arrive(side=side):
                outw_move("y", side, step, 1 - g).wait_recv()
                outw_move("1", side, step, 1 - g).start()

            when(present(side, step), arrive)

    last = planes - 1
    work(total // 2)
    for cut in range(cuts):
        tok_relay(1, cut)
        work(total // 4 // cuts)
    wy_copies = []
    for step in range(1, count):
        w_copies[step - 1].wait_recv()
        came = weight_rows((k + count - step) % count, g)
        wy_copies.append(
            launch(remote(came, came, w_y_send.at[step], w_y_recv.at[step], at(group=1 - g)))
        )
        work(1)
    for step in range(2, planes):
        for cut in range(cuts):
            if step == planes - 1:
                break
            tok_relay(step, cut)
            tok_cross(step - 1, cut)
            work(1)
    work(total)
    for copy in locals_[2:]:
        copy.wait()
    for copy in wy_copies:
        copy.wait_recv()

    def stand(index, carry):
        place = pl.ds(pl.multiple_of(index * TILE, TILE), TILE)
        for s in range(3):
            wide[s * chans : (s + 1) * chans, place] = (
                raw[s, place, :].astype(jnp.float32).T.astype(jnp.bfloat16)
            )
        return carry

    lax.fori_loop(0, raw.shape[1] // TILE, stand, 0)
    core_own.wait_recv()

    def ends(side):
        return z + 2 == planes if side == 0 else z == 1

    for side in range(2):
        outw_hop(side, 1, jnp.logical_not(ends(side)))
    for cut in range(cuts):
        tok_relay(last, cut)
        if last > 1:
            tok_cross(last - 1, cut)
        if cut == 0:
            project(k, 0)
            project(other, 0)
        elif cut == 1:
            for step in range(1, last - 1):
                tok_done(step)
    for side in range(2):
        outw_hop(side, 1, ends(side))
    tok_done(last - 1)
    for cut in range(cuts):
        tok_cross(last, cut)
    tok_done(last)
    outw_relay(1)

    groups = chans // 16 // parts

    def filter_step(index, carry):
        filter_group(index, streams, taps, keep, bands, mixed, chans)
        return carry

    m_copies = []
    for part in range(parts):
        lax.fori_loop(part * groups, (part + 1) * groups, filter_step, 0)
        span = pl.ds(part * groups * 16, groups * 16)
        for step in range(1, count):
            to = (k + step) % count
            m_copies.append(
                launch(
                    remote(
                        mixed.at[pl.ds(2 * to, 2), span, :],
                        arrived.at[k, :, span, :],
                        m_send.at[part, step],
                        m_recv.at[part, step],
                        at(ctx=to),
                    )
                )
            )
        if part == 1:
            for step in range(2, last):
                outw_relay(step)
        if part == 2:
            outw_last(1)
    own_mixed = pltpu.make_async_copy(
        mixed.at[pl.ds(2 * k, 2)], arrived.at[k], local_sem.at[0]
    )
    own_mixed.start()
    own_mixed.wait()
    for copy in m_copies:
        copy.wait_recv()
    for owner in range(count):
        for h in range(2):
            turned[h, :, owner * chans : (owner + 1) * chans] = (
                arrived[owner, h].astype(jnp.float32).T.astype(jnp.bfloat16)
            )

    wide_e = outw_ref.shape[1]

    def give(owner, side, step, side_core):
        copy = remote(
            sent_part.at[owner],
            got_part.at[owner],
            p_send.at[side, step, side_core],
            p_recv.at[side, step, side_core],
            at(chan=1 - x),
        )
        return copy

    def multiply(owner):
        sent_part[owner] = jnp.dot(
            turned[1 - x], outw[owner], preferred_element_type=jnp.float32
        ).astype(jnp.bfloat16)

    def keep_own(owner):
        own_part[owner] = jnp.dot(
            turned[x], outw[owner], preferred_element_type=jnp.float32
        )

    def finish(owner):
        span = pl.ds(pl.multiple_of(owner * wide_e, TILE), wide_e)
        out_ref[:, span] = (own_part[owner] + got_part[owner].astype(jnp.float32)).astype(
            jnp.bfloat16
        )

    def pair_of(side, step):
        return [2 * (origin(side, step) // 2) + c for c in range(2)]

    def each(step, action):
        for side in range(2):
            if step == 0:
                if side == 0:
                    action(side, step)
                continue

            def go(side=side):
                action(side, step)

            when(present(side, step), go)

    def send_part(side, step):
        for kind in range(2):
            if step:
                half = g if kind == 0 else 1 - g
                outw_move(str(kind), side, step, half).wait_recv()
        for c, owner in enumerate(pair_of(side, step)):
            multiply(owner)
            give(owner, side, step, c).start()

    def own_dots(side, step):
        for owner in pair_of(side, step):
            keep_own(owner)

    def take_part(side, step):
        for c, owner in enumerate(pair_of(side, step)):
            give(owner, side, step, c).wait_recv()
            finish(owner)

    def part_gone(side, step):
        for c, owner in enumerate(pair_of(side, step)):
            give(owner, side, step, c).wait_send()

    core_own_o.wait_recv()
    for step in range(2):
        each(step, send_part)
    outw_relay(last)
    for step in range(2, last):
        outw_last(step)
        each(step, send_part)
    for step in range(last):
        each(step, own_dots)
    outw_last(last)
    each(last, send_part)
    each(last, own_dots)
    for step in range(planes):
        each(step, take_part)
    for step in range(planes):
        each(step, part_gone)

    for copy in flights:
        copy.wait_send()
    for ready, make in guarded:

        def left(make=make):
            make().wait_send()

        when(ready, left)
    for step in range(1, planes):
        for side in range(2):

            def gone(side=side, step=step):
                for cut in range(cuts):
                    tok_x(side, step, x, cut).wait_send()
                    tok_c(side, step, x, 0, cut).wait_send()
                    tok_c(side, step, 1 - x, 1, cut).wait_send()
                outw_move("y", side, step, g).wait_send()
                outw_move("0", side, step, g).wait_send()
                outw_move("1", side, step, 1 - g).wait_send()

            when(present(side, step), gone)


CUTS = 4
PARTS = 4


def fused(tokens, in_weight, short_taps, filters, doc_lengths, out_weight):
    count = lax.axis_size("ctx")
    chans = in_weight.shape[2] // count
    rows, model = tokens.shape
    seq_len = filters.shape[1] * count
    blocks = seq_len // TILE
    planes = count // 2
    dma = pltpu.SemaphoreType.DMA
    anywhere = pl.BlockSpec(memory_space=pl.ANY)
    vmem = pl.BlockSpec(memory_space=pltpu.VMEM)
    return pl.pallas_call(
        functools.partial(exchange_kernel, planes, CUTS, PARTS),
        out_shape=jax.ShapeDtypeStruct((rows // 2, model), jnp.bfloat16),
        in_specs=[anywhere] * 4 + [vmem, pl.BlockSpec(memory_space=pltpu.SMEM)],
        out_specs=vmem,
        scratch_shapes=[
            pltpu.VMEM((count, rows, model), jnp.bfloat16),
            pltpu.VMEM((3, model, chans), jnp.bfloat16),
            pltpu.VMEM((3 * chans, model), jnp.bfloat16),
            pltpu.VMEM((chans, seq_len), jnp.bfloat16),
            pltpu.VMEM((count,) + out_weight.shape, jnp.bfloat16),
            pltpu.VMEM((3, blocks, chans, TILE), jnp.float32),
            pltpu.VMEM((chans, seq_len), jnp.float32),
            pltpu.VMEM((chans // 4, blocks // 2, 2 * TILE, 2 * TILE), jnp.bfloat16),
            pltpu.VMEM((blocks, chans, TILE), jnp.bfloat16),
            pltpu.VMEM((count, 2, chans, TILE), jnp.bfloat16),
            pltpu.VMEM((2, TILE, count * chans), jnp.bfloat16),
            pltpu.VMEM((count, TILE, out_weight.shape[1]), jnp.float32),
            pltpu.VMEM((count, TILE, out_weight.shape[1]), jnp.bfloat16),
            pltpu.VMEM((count, TILE, out_weight.shape[1]), jnp.bfloat16),
            pltpu.VMEM((9, chans, TILE), jnp.float32),
            pltpu.VMEM((2, blocks, 8, TILE), jnp.float32),
            dma((6,)),
            dma((2,)),
            dma((2,)),
        ]
        + [dma((2, planes, CUTS))] * 4
        + [dma((2, 2, planes, CUTS))] * 2
        + [dma((count,))] * 8
        + [dma((2, planes))] * 4
        + [dma((2, 2, planes))] * 2
        + [dma((PARTS, count))] * 2
        + [dma((2, planes, 2))] * 2,
        compiler_params=pltpu.CompilerParams(
            collective_id=0, has_side_effects=True, vmem_limit_bytes=61 * 1024 * 1024
        ),
    )(in_weight.transpose(1, 0, 2), filters, tokens, out_weight, short_taps, doc_lengths)


def fits(tokens, in_weight, filters, out_weight):
    count = lax.axis_size("ctx")
    rows, model = tokens.shape
    return (
        count % 2 == 0
        and count >= 6
        and lax.axis_size("chan") == 2
        and lax.axis_size("groups") == 2
        and in_weight.shape[0] == 2 * TILE
        and in_weight.shape[2] == count * TILE
        and filters.shape[1] == 2 * TILE
        and rows == 2 * TILE
        and out_weight.shape[1] == 2 * TILE
        and model == 2 * TILE * count
        and count * rows * model * 2 <= 8 * 1024 * 1024
    )


def layer(tokens, in_weight, short_taps, filters, doc_lengths, out_weight):
    if fits(tokens, in_weight, filters, out_weight):
        return fused(tokens, in_weight, short_taps, filters, doc_lengths, out_weight)
    return shards(tokens, in_weight, short_taps, filters, doc_lengths, out_weight)


def solution(mesh):
    placed = (
        P(("groups", "ctx"), None),
        P("ctx", None, "chan"),
        P(None, None, "chan"),
        P("chan", "ctx"),
        P("groups"),
        P("chan", "ctx"),
    )
    return jax.shard_map(
        layer,
        mesh=mesh,
        in_specs=placed,
        out_specs=P(("groups", "ctx", "chan"), None),
        check_vma=False,
    )
```

```python
import functools
import math

import jax
import jax.numpy as jnp
from jax import lax
from jax.experimental import pallas as pl
from jax.experimental.pallas import tpu as pltpu
from jax.sharding import PartitionSpec as P

def contract(form, left, right):
    return jnp.einsum(form, left, right, precision=lax.Precision.HIGHEST)


def angle_table(rows, cols, period):
    product = lax.broadcasted_iota(jnp.int32, (rows, cols), 0) * lax.broadcasted_iota(
        jnp.int32, (rows, cols), 1
    )
    theta = (product % period).astype(jnp.float32) * (2.0 * math.pi / period)
    return (jnp.cos(theta), jnp.sin(theta))


def document_ids(doc_lengths, seq_len):
    count = doc_lengths.shape[0]
    order = lax.broadcasted_iota(jnp.int32, (count, count), 0)
    before = order >= lax.broadcasted_iota(jnp.int32, (count, count), 1)
    ends = jnp.sum(jnp.where(before, doc_lengths[None, :], 0), axis=1)
    places = lax.broadcasted_iota(jnp.int32, (seq_len, ends.shape[0]), 0)
    return jnp.sum((places >= ends[None, :]).astype(jnp.int32), axis=1)


def short_conv(streams, taps, doc_id):
    result = taps[:, 0, :, None] * streams
    for lag in (1, 2):
        moved = jnp.pad(streams, ((0, 0), (0, 0), (lag, 0)))[:, :, :-lag]
        linked = jnp.concatenate((jnp.zeros((lag,), bool), doc_id[lag:] == doc_id[:-lag]))
        result = result + taps[:, lag, :, None] * jnp.where(linked[None, None, :], moved, 0.0)
    return result


def causal_filter(gated, kernel_rows):
    count, seq_len = gated.shape
    width = math.gcd(seq_len, 128)
    half = seq_len // width
    span = 2 * half
    total = span * width
    signal = gated.reshape(count, half, width)
    kernel = kernel_rows.reshape(count, half, width)
    cos_b, sin_b = angle_table(span, span, span)
    twist_c, twist_s = angle_table(span, width, total)
    cos_a, sin_a = angle_table(width, width, width)

    def forward(values):
        padded = jnp.concatenate((values, jnp.zeros_like(values)), 1)
        real_part = contract("kb,cba->cka", cos_b, padded)
        imag_part = -contract("kb,cba->cka", sin_b, padded)
        turned_r = real_part * twist_c + imag_part * twist_s
        turned_i = imag_part * twist_c - real_part * twist_s
        spec_r = contract("cka,aj->ckj", turned_r, cos_a) + contract("cka,aj->ckj", turned_i, sin_a)
        spec_i = contract("cka,aj->ckj", turned_i, cos_a) - contract("cka,aj->ckj", turned_r, sin_a)
        return (spec_r, spec_i)

    sig_r, sig_i = forward(signal)
    ker_r, ker_i = forward(kernel)
    prod_r = sig_r * ker_r - sig_i * ker_i
    prod_i = sig_r * ker_i + sig_i * ker_r
    back_r = contract("ckj,aj->cka", prod_r, cos_a) - contract("ckj,aj->cka", prod_i, sin_a)
    back_i = contract("ckj,aj->cka", prod_i, cos_a) + contract("ckj,aj->cka", prod_r, sin_a)
    untwist_r = back_r * twist_c - back_i * twist_s
    untwist_i = back_i * twist_c + back_r * twist_s
    blocks = contract("bk,cka->cba", cos_b, untwist_r) - contract("bk,cka->cba", sin_b, untwist_i)
    blocks = blocks[:, :half]
    return (blocks / total).reshape(count, seq_len)


def shards(tokens, in_weight, short_taps, filters, doc_lengths, out_weight):
    width_dev = in_weight.shape[2]
    group_width = width_dev // lax.axis_size("ctx")
    streams = jnp.einsum(
        "dsc,td->sct",
        lax.all_gather(in_weight, "ctx", axis=0, tiled=True),
        tokens,
        preferred_element_type=jnp.float32,
    )
    packed = jnp.concatenate((streams.astype(jnp.bfloat16), filters[None]), 0)
    spread = lax.all_to_all(packed, "ctx", split_axis=1, concat_axis=2, tiled=True)
    taps = lax.dynamic_slice_in_dim(
        short_taps, lax.axis_index("ctx") * group_width, group_width, 2
    ).astype(jnp.float32)
    seq_len = spread.shape[2]
    doc_id = document_ids(doc_lengths, seq_len)
    conv = short_conv(spread[:3].astype(jnp.float32), taps, doc_id)
    filtered = causal_filter(conv[0] * conv[2], spread[3].astype(jnp.float32))
    mixed = (conv[1] * filtered).astype(jnp.bfloat16)
    returned = lax.all_to_all(mixed, "ctx", split_axis=1, concat_axis=0, tiled=True)
    partial_out = lax.dot_general(
        returned,
        lax.all_gather(out_weight, "ctx", axis=1, tiled=True),
        (((0,), (0,)), ((), ())),
        preferred_element_type=jnp.float32,
    )
    return lax.psum_scatter(partial_out, "chan", scatter_dimension=0, tiled=True).astype(
        jnp.bfloat16
    )


TILE = 128
HALF = 64
THICK = 16
MESH = pl.DeviceIdType.MESH


def spread_taps(taps_ref, taps, chans, me):
    for s in range(3):
        rows = taps_ref[s, :, pl.ds(pl.multiple_of(me * chans, TILE), chans)].astype(jnp.float32)
        for lag in range(3):
            taps[3 * s + lag] = jnp.broadcast_to(rows[lag : lag + 1, :], (TILE, chans)).T


def mark_links(docs_ref, keep, blocks):
    lane = lax.broadcasted_iota(jnp.int32, (8, TILE), 1)
    ends = []
    for j in range(docs_ref.shape[0]):
        ends.append(docs_ref[j] + ends[-1] if j else docs_ref[j])
    for b in range(blocks):
        place = lane + b * TILE
        for lag in (1, 2):
            linked = place >= lag
            for end in ends:
                linked = jnp.logical_and(
                    linked, jnp.logical_or(place < end, place - lag >= end)
                )
            keep[lag - 1, b] = linked.astype(jnp.float32)


def build_band(index, kernels, bands):
    seq = kernels.shape[1]
    lane = lax.broadcasted_iota(jnp.int32, (THICK, TILE), 1)
    place = lane % HALF - lax.broadcasted_iota(jnp.int32, (THICK, TILE), 0)
    low = lane < HALF
    for pair in range(2):
        rows = [
            jnp.broadcast_to(kernels[pl.ds(4 * index + 2 * pair + u, 1), :], (THICK, seq))
            for u in range(2)
        ]
        for q in range(TILE // THICK):
            moved = [
                pltpu.roll(
                    rows[u],
                    (seq - HALF * (1 - u) + q * THICK) % seq,
                    1,
                    stride=1,
                    stride_axis=0,
                )
                for u in range(2)
            ]
            for m in range(seq // TILE):
                span = slice(m * TILE, (m + 1) * TILE)
                tile = jnp.where(low, moved[0][:, span], moved[1][:, span])
                if m == 0:
                    tile = jnp.where(place + HALF >= q * THICK, tile, 0.0)
                first = (m % 2) * TILE + q * THICK
                bands[
                    index, m // 2, first : first + THICK, pair * TILE : (pair + 1) * TILE
                ] = tile.astype(jnp.bfloat16)


def filter_group(index, streams, taps, keep, bands, mixed, chans):
    blocks = keep.shape[1]
    lane = lax.broadcasted_iota(jnp.int32, (8, TILE), 1)
    sub = lax.broadcasted_iota(jnp.int32, (8, TILE), 0)
    left, top = lane < HALF, sub < 4
    second = (sub & 2) > 0
    straight = ((sub & 1) == 0) != top
    products = []
    for half in range(2):
        first = pl.multiple_of(index * 16 + 8 * half, 8)
        rows = pl.ds(first, 8)
        conv = [None] * 3
        for s in range(3):
            tap = [taps[3 * s + lag, rows, :] for lag in range(3)]
            conv[s] = []
            before = [None, None]
            for b in range(blocks):
                value = streams[s, b, rows, :]
                total = tap[0] * value
                for lag in (1, 2):
                    rolled = pltpu.roll(value, lag, 1)
                    moved = rolled
                    if b:
                        moved = jnp.where(lane < lag, before[lag - 1], rolled)
                    before[lag - 1] = rolled
                    total = total + tap[lag] * (keep[lag - 1, b] * moved)
                conv[s].append(total)
        gated = [conv[0][b] * conv[2][b] for b in range(blocks)]
        turned = [pltpu.roll(gated[b], HALF, 1) for b in range(blocks)]
        late = [
            jnp.where(left, turned[b - 1] if b else 0.0, turned[b]) for b in range(blocks)
        ]
        packed = []
        for quad in range(2):
            if quad == 0:
                rows_of = [
                    jnp.where(top, gated[b], pltpu.roll(late[b], 4, 0)) for b in range(blocks)
                ]
            else:
                rows_of = [
                    jnp.where(top, pltpu.roll(gated[b], 4, 0), late[b]) for b in range(blocks)
                ]
            now = jnp.concatenate(rows_of, axis=0).astype(jnp.bfloat16)
            old = jnp.concatenate(
                [jnp.zeros_like(rows_of[0])] + rows_of[:-1], axis=0
            ).astype(jnp.bfloat16)
            packed.append(jnp.concatenate([now, old], axis=1))
        straights, swapped = [], []
        for quad in range(2):
            which = 4 * index + 2 * half + quad
            sums = [None] * blocks
            for t in range(blocks // 2):
                height = 8 * blocks - 16 * t
                part = jnp.dot(
                    packed[quad][:height], bands[which, t], preferred_element_type=jnp.float32
                )
                for b in range(2 * t, blocks):
                    piece = part[8 * (b - 2 * t) : 8 * (b - 2 * t) + 8]
                    sums[b] = piece if sums[b] is None else sums[b] + piece
            one, two = [], []
            for b in range(blocks):
                both = jnp.where(second, sums[b][:, TILE:], sums[b][:, :TILE])
                both = jnp.where(straight, both, pltpu.roll(both, HALF, 1))
                one.append(both)
                two.append(pltpu.roll(both, 4, 0))
            straights.append(one)
            swapped.append(two)
        result = []
        for b in range(blocks):
            upper = jnp.where(left, swapped[0][b], straights[0][b])
            lower = jnp.where(left, straights[1][b], swapped[1][b])
            result.append(conv[1][b] * jnp.where(top, upper, lower))
        products.append(result)
    for b in range(blocks):
        mixed[b, pl.ds(pl.multiple_of(index * 16, 16), 16), :] = jnp.concatenate(
            [products[0][b], products[1][b]], axis=0
        ).astype(jnp.bfloat16)


def exchange_kernel(
    planes,
    cuts,
    parts,
    weight_ref,
    filters_ref,
    tokens_ref,
    outw_ref,
    taps_ref,
    docs_ref,
    out_ref,
    toks,
    raw,
    wide,
    lags,
    outw,
    streams,
    kernels,
    bands,
    mixed,
    arrived,
    turned,
    own_part,
    sent_part,
    got_part,
    taps,
    keep,
    local_sem,
    own_send,
    own_recv,
    tok_z_send,
    tok_z_recv,
    tok_x_send,
    tok_x_recv,
    tok_c_send,
    tok_c_recv,
    w_send,
    w_recv,
    w_y_send,
    w_y_recv,
    f_send,
    f_recv,
    f_y_send,
    f_y_recv,
    o_z_send,
    o_z_recv,
    o_y_send,
    o_y_recv,
    o_c_send,
    o_c_recv,
    m_send,
    m_recv,
    p_send,
    p_recv,
):
    g = lax.axis_index("groups")
    k = lax.axis_index("ctx")
    x = lax.axis_index("chan")
    z, core = k // 2, k % 2
    count = 2 * planes
    blocks = 2 * count
    rows = tokens_ref.shape[0]
    lanes = rows // 2
    piece = lanes // cuts
    depth = weight_ref.shape[1]
    half_d = depth // 2
    half_o = outw_ref.shape[0] // 2
    chans = kernels.shape[0]
    other = 2 * z + 1 - core

    def at(group=g, ctx=k, chan=x):
        return (group, ctx, chan)

    def remote(src, dst, send, recv, where):
        return pltpu.make_async_remote_copy(
            src_ref=src,
            dst_ref=dst,
            send_sem=send,
            recv_sem=recv,
            device_id=where,
            device_id_type=MESH,
        )

    def tile_of(index):
        return pl.ds(pl.multiple_of(index * TILE, TILE), TILE)

    def when(condition, action):
        pl.when(condition)(action)

    barrier = pltpu.get_barrier_semaphore()
    for step in range(1, count):
        pl.semaphore_signal(
            barrier, inc=1, device_id=at(ctx=(k + step) % count), device_id_type=MESH
        )
    pl.semaphore_signal(barrier, inc=1, device_id=at(chan=1 - x), device_id_type=MESH)
    pl.semaphore_signal(barrier, inc=1, device_id=at(group=1 - g), device_id_type=MESH)
    pl.semaphore_wait(barrier, count + 1)

    def lag_column(owner, half):
        return lags.at[:, tile_of(2 * owner + half)]

    def lags_of(owner, half):
        return filters_ref.at[tile_of(owner), tile_of(half)]

    def weight_rows(owner, half):
        return raw.at[:, pl.ds(pl.multiple_of(owner * depth + half * half_d, TILE), half_d), :]

    def weight_of(owner, half):
        return weight_ref.at[:, pl.ds(pl.multiple_of(half * half_d, TILE), half_d), tile_of(owner)]

    def tok(owner, half, cut):
        return toks.at[owner, pl.ds(pl.multiple_of(half * lanes + cut * piece, piece), piece), :]

    def outw_at(owner, half):
        return outw.at[owner, pl.ds(pl.multiple_of(half * half_o, half_o), half_o), :]

    flights = []

    def launch(copy):
        copy.start()
        flights.append(copy)
        return copy

    f_copies = [
        launch(
            remote(
                lags_of((k + step) % count, g),
                lag_column(k, g),
                f_send.at[step],
                f_recv.at[step],
                at(ctx=(k + step) % count),
            )
        )
        for step in range(1, count)
    ]

    locals_ = [
        pltpu.make_async_copy(lags_of(k, 0), lag_column(k, 0), local_sem.at[0]),
        pltpu.make_async_copy(lags_of(k, 1), lag_column(k, 1), local_sem.at[1]),
        pltpu.make_async_copy(weight_of(k, 0), weight_rows(k, 0), local_sem.at[2]),
        pltpu.make_async_copy(weight_of(k, 1), weight_rows(k, 1), local_sem.at[3]),
        pltpu.make_async_copy(tokens_ref, toks.at[k], local_sem.at[4]),
        pltpu.make_async_copy(outw_ref, outw.at[k], local_sem.at[5]),
    ]
    for copy in locals_[:2]:
        copy.start()

    guarded = []

    def present(side, step):
        return z >= step if side == 0 else z + step < planes

    def onward(side):
        return z + 1 < planes if side == 0 else z >= 1

    def origin(side, step):
        return 2 * (z - step if side == 0 else z + step) + core

    def beyond(side):
        return at(ctx=2 * (z + 1 if side == 0 else z - 1) + core)

    def hop(side, step, make, only=None):
        ready = onward(side)
        if only is not None:
            ready = jnp.logical_and(ready, only)
        if step > 1:
            ready = jnp.logical_and(ready, present(side, step - 1))

        def go():
            make().start()

        when(ready, go)
        guarded.append((ready, make))

    def tok_hop(side, step, cut):
        def make():
            if step == 1:
                source = tokens_ref.at[
                    pl.ds(pl.multiple_of(x * lanes + cut * piece, piece), piece), :
                ]
            else:
                source = tok(origin(side, step - 1), x, cut)
            return remote(
                source,
                tok(origin(side, step - 1), x, cut),
                tok_z_send.at[side, step, cut],
                tok_z_recv.at[side, step, cut],
                beyond(side),
            )

        hop(side, step, make)

    for cut in range(cuts):
        for side in range(2):
            tok_hop(side, 1, cut)

    w_copies = [
        launch(
            remote(
                weight_of((k + step) % count, g),
                weight_rows(k, g),
                w_send.at[step],
                w_recv.at[step],
                at(ctx=(k + step) % count),
            )
        )
        for step in range(1, count)
    ]
    for copy in locals_[2:]:
        copy.start()
    core_own = launch(
        remote(tokens_ref, toks.at[k], own_send.at[0], own_recv.at[0], at(ctx=other))
    )
    core_own_o = launch(
        remote(outw_ref, outw.at[k], own_send.at[1], own_recv.at[1], at(ctx=other))
    )

    spread_taps(taps_ref, taps, chans, k)
    mark_links(docs_ref, keep, blocks)

    fy_copies = []
    for step in range(1, count):
        f_copies[step - 1].wait_recv()
        came = lag_column((k + count - step) % count, g)
        fy_copies.append(
            launch(remote(came, came, f_y_send.at[step], f_y_recv.at[step], at(group=1 - g)))
        )
    for copy in fy_copies:
        copy.wait_recv()
    for copy in locals_[:2]:
        copy.wait()
    kernels[...] = lags[...].astype(jnp.float32)

    total = bands.shape[0]
    done = [0]

    def work(amount):
        first, last = done[0], min(done[0] + amount, total)
        done[0] = last

        def body(index, carry):
            build_band(index, kernels, bands)
            return carry

        if last > first:
            lax.fori_loop(first, last, body, 0)

    def tok_z(side, step, cut):
        came = tok(origin(side, step), x, cut)
        return remote(
            came, came, tok_z_send.at[side, step, cut], tok_z_recv.at[side, step, cut], at(ctx=other)
        )

    def tok_x(side, step, half, cut):
        came = tok(origin(side, step), half, cut)
        return remote(
            came, came, tok_x_send.at[side, step, cut], tok_x_recv.at[side, step, cut], at(chan=1 - x)
        )

    def tok_c(side, step, half, which, cut):
        came = tok(origin(side, step), half, cut)
        return remote(
            came,
            came,
            tok_c_send.at[which, side, step, cut],
            tok_c_recv.at[which, side, step, cut],
            at(ctx=other),
        )

    def tok_relay(step, cut):
        for side in range(2):

            def arrive(side=side):
                tok_z(side, step, cut).wait_recv()

            when(present(side, step), arrive)
            if step + 1 < planes:
                tok_hop(side, step + 1, cut)

            def share(side=side):
                tok_x(side, step, x, cut).start()
                tok_c(side, step, x, 0, cut).start()

            when(present(side, step), share)

    def tok_cross(step, cut):
        for side in range(2):

            def arrive(side=side):
                tok_x(side, step, 1 - x, cut).wait_recv()
                tok_c(side, step, 1 - x, 1, cut).start()

            when(present(side, step), arrive)

    def project(index, carry):
        value = lax.dot_general(
            wide[...],
            toks[index],
            (((1,), (1,)), ((), ())),
            preferred_element_type=jnp.float32,
        )
        value = value.astype(jnp.bfloat16).astype(jnp.float32)
        for s in range(3):
            for h in range(2):
                streams[s, 2 * index + h] = value[
                    s * chans : (s + 1) * chans, h * TILE : (h + 1) * TILE
                ]
        return carry

    def tok_done(step):
        for side in range(2):

            def arrive(side=side):
                for cut in range(cuts):
                    for which in range(2):
                        tok_c(side, step, which, which, cut).wait_recv()

                def both(index, carry):
                    return project(2 * (origin(side, step) // 2) + index, carry)

                lax.fori_loop(0, 2, both, 0)

            when(present(side, step), arrive)

    def outw_hop(side, step, only=None):
        def make():
            if step == 1:
                source = outw_ref.at[pl.ds(pl.multiple_of(g * half_o, half_o), half_o), :]
            else:
                source = outw_at(origin(side, step - 1), g)
            return remote(
                source,
                outw_at(origin(side, step - 1), g),
                o_z_send.at[side, step],
                o_z_recv.at[side, step],
                beyond(side),
            )

        hop(side, step, make, only)

    def outw_move(kind, side, step, half):
        came = outw_at(origin(side, step), half)
        if kind == "z":
            sems, where = (o_z_send.at[side, step], o_z_recv.at[side, step]), at(ctx=other)
        elif kind == "y":
            sems, where = (o_y_send.at[side, step], o_y_recv.at[side, step]), at(group=1 - g)
        else:
            which = int(kind)
            sems = (o_c_send.at[which, side, step], o_c_recv.at[which, side, step])
            where = at(ctx=other)
        return remote(came, came, sems[0], sems[1], where)

    middle = jnp.logical_and(z >= 1, z + 1 < planes)

    def outw_relay(step, who):
        for side in range(2):
            here = jnp.logical_and(present(side, step), who)

            def arrive(side=side):
                outw_move("z", side, step, g).wait_recv()

            when(here, arrive)
            if step + 1 < planes:
                outw_hop(side, step + 1, who)

            def share(side=side):
                outw_move("y", side, step, g).start()
                outw_move("0", side, step, g).start()

            when(here, share)

    def outw_last(step):
        for side in range(2):

            def arrive(side=side):
                outw_move("y", side, step, 1 - g).wait_recv()
                outw_move("1", side, step, 1 - g).start()

            when(present(side, step), arrive)

    last = planes - 1
    work(total // 4)
    for cut in range(cuts):
        tok_relay(1, cut)
        work(total // 4 // cuts)
    wy_copies = []
    for step in range(1, count):
        w_copies[step - 1].wait_recv()
        came = weight_rows((k + count - step) % count, g)
        wy_copies.append(
            launch(remote(came, came, w_y_send.at[step], w_y_recv.at[step], at(group=1 - g)))
        )
        work(1)
    for step in range(2, planes):
        for cut in range(cuts):
            if step == planes - 1:
                break
            tok_relay(step, cut)
            tok_cross(step - 1, cut)
            work(2)
    work(total)
    for copy in locals_[2:]:
        copy.wait()
    for copy in wy_copies:
        copy.wait_recv()

    def stand(index, carry):
        place = pl.ds(pl.multiple_of(index * TILE, TILE), TILE)
        for s in range(3):
            wide[s * chans : (s + 1) * chans, place] = (
                raw[s, place, :].astype(jnp.float32).T.astype(jnp.bfloat16)
            )
        return carry

    lax.fori_loop(0, raw.shape[1] // TILE, stand, 0)
    core_own.wait_recv()

    def ends(side):
        return z + 2 == planes if side == 0 else z == 1

    for side in range(2):
        outw_hop(side, 1, jnp.logical_not(ends(side)))
    for cut in range(cuts):
        tok_relay(last, cut)
        if last > 1:
            tok_cross(last - 1, cut)
        if cut == 0:
            project(k, 0)
            project(other, 0)
        elif cut == 1:
            for step in range(1, last - 1):
                tok_done(step)
    for side in range(2):
        outw_hop(side, 1, ends(side))
    outer = jnp.logical_not(middle)
    outw_relay(1, middle)
    tok_done(last - 1)
    for cut in range(cuts):
        tok_cross(last, cut)
    for step in range(2, last):
        outw_relay(step, middle)
    tok_done(last)
    outw_relay(1, outer)

    groups = chans // 16 // parts

    def filter_step(index, carry):
        filter_group(index, streams, taps, keep, bands, mixed, chans)
        return carry

    m_copies = []
    for part in range(parts):
        lax.fori_loop(part * groups, (part + 1) * groups, filter_step, 0)
        span = pl.ds(part * groups * 16, groups * 16)
        for step in range(1, count):
            to = (k + step) % count
            m_copies.append(
                launch(
                    remote(
                        mixed.at[2 * to + 1 - x, span, :],
                        arrived.at[k, 1 - x, span, :],
                        m_send.at[part, step],
                        m_recv.at[part, step],
                        at(ctx=to),
                    )
                )
            )
        if part == 1:
            for step in range(2, last):
                outw_relay(step, outer)
        if part == 2:
            outw_last(1)
    own_mixed = pltpu.make_async_copy(
        mixed.at[pl.ds(2 * k, 2)], arrived.at[k], local_sem.at[0]
    )
    own_mixed.start()
    late_copies = [
        launch(
            remote(
                mixed.at[2 * ((k + step) % count) + x],
                arrived.at[k, x],
                m_send.at[parts, step],
                m_recv.at[parts, step],
                at(ctx=(k + step) % count),
            )
        )
        for step in range(1, count)
    ]
    own_mixed.wait()

    def stand_rows(h):
        for owner in range(count):
            turned[h, :, owner * chans : (owner + 1) * chans] = (
                arrived[owner, h].astype(jnp.float32).T.astype(jnp.bfloat16)
            )

    for copy in m_copies:
        copy.wait_recv()
    stand_rows(1 - x)

    wide_e = outw_ref.shape[1]

    def give(owner, side, step, side_core):
        copy = remote(
            sent_part.at[owner],
            got_part.at[owner],
            p_send.at[side, step, side_core],
            p_recv.at[side, step, side_core],
            at(chan=1 - x),
        )
        return copy

    def multiply(owner):
        sent_part[owner] = jnp.dot(
            turned[1 - x], outw[owner], preferred_element_type=jnp.float32
        ).astype(jnp.bfloat16)

    def keep_own(owner):
        own_part[owner] = jnp.dot(
            turned[x], outw[owner], preferred_element_type=jnp.float32
        )

    def finish(owner):
        span = pl.ds(pl.multiple_of(owner * wide_e, TILE), wide_e)
        out_ref[:, span] = (own_part[owner] + got_part[owner].astype(jnp.float32)).astype(
            jnp.bfloat16
        )

    def pair_of(side, step):
        return [2 * (origin(side, step) // 2) + c for c in range(2)]

    def each(step, action):
        for side in range(2):
            if step == 0:
                if side == 0:
                    action(side, step)
                continue

            def go(side=side):
                action(side, step)

            when(present(side, step), go)

    def send_part(side, step):
        for kind in range(2):
            if step:
                half = g if kind == 0 else 1 - g
                outw_move(str(kind), side, step, half).wait_recv()
        for c, owner in enumerate(pair_of(side, step)):
            multiply(owner)
            give(owner, side, step, c).start()

    def own_dots(side, step):
        for owner in pair_of(side, step):
            keep_own(owner)

    def take_part(side, step):
        for c, owner in enumerate(pair_of(side, step)):
            give(owner, side, step, c).wait_recv()
            finish(owner)

    def part_gone(side, step):
        for c, owner in enumerate(pair_of(side, step)):
            give(owner, side, step, c).wait_send()

    core_own_o.wait_recv()
    for step in range(2):
        each(step, send_part)
    outw_relay(last, outer)
    for step in range(2, last):
        outw_last(step)
        each(step, send_part)
    for copy in late_copies:
        copy.wait_recv()
    stand_rows(x)
    for step in range(last):
        each(step, own_dots)
    outw_last(last)
    each(last, send_part)
    each(last, own_dots)
    for step in range(planes):
        each(step, take_part)
    for step in range(planes):
        each(step, part_gone)

    for copy in flights:
        copy.wait_send()
    for ready, make in guarded:

        def left(make=make):
            make().wait_send()

        when(ready, left)
    for step in range(1, planes):
        for side in range(2):

            def gone(side=side, step=step):
                for cut in range(cuts):
                    tok_x(side, step, x, cut).wait_send()
                    tok_c(side, step, x, 0, cut).wait_send()
                    tok_c(side, step, 1 - x, 1, cut).wait_send()
                outw_move("y", side, step, g).wait_send()
                outw_move("0", side, step, g).wait_send()
                outw_move("1", side, step, 1 - g).wait_send()

            when(present(side, step), gone)


CUTS = 4
PARTS = 4


def fused(tokens, in_weight, short_taps, filters, doc_lengths, out_weight):
    count = lax.axis_size("ctx")
    chans = in_weight.shape[2] // count
    rows, model = tokens.shape
    seq_len = filters.shape[1] * count
    blocks = seq_len // TILE
    planes = count // 2
    dma = pltpu.SemaphoreType.DMA
    anywhere = pl.BlockSpec(memory_space=pl.ANY)
    vmem = pl.BlockSpec(memory_space=pltpu.VMEM)
    return pl.pallas_call(
        functools.partial(exchange_kernel, planes, CUTS, PARTS),
        out_shape=jax.ShapeDtypeStruct((rows // 2, model), jnp.bfloat16),
        in_specs=[anywhere] * 4 + [vmem, pl.BlockSpec(memory_space=pltpu.SMEM)],
        out_specs=vmem,
        scratch_shapes=[
            pltpu.VMEM((count, rows, model), jnp.bfloat16),
            pltpu.VMEM((3, model, chans), jnp.bfloat16),
            pltpu.VMEM((3 * chans, model), jnp.bfloat16),
            pltpu.VMEM((chans, seq_len), jnp.bfloat16),
            pltpu.VMEM((count,) + out_weight.shape, jnp.bfloat16),
            pltpu.VMEM((3, blocks, chans, TILE), jnp.float32),
            pltpu.VMEM((chans, seq_len), jnp.float32),
            pltpu.VMEM((chans // 4, blocks // 2, 2 * TILE, 2 * TILE), jnp.bfloat16),
            pltpu.VMEM((blocks, chans, TILE), jnp.bfloat16),
            pltpu.VMEM((count, 2, chans, TILE), jnp.bfloat16),
            pltpu.VMEM((2, TILE, count * chans), jnp.bfloat16),
            pltpu.VMEM((count, TILE, out_weight.shape[1]), jnp.float32),
            pltpu.VMEM((count, TILE, out_weight.shape[1]), jnp.bfloat16),
            pltpu.VMEM((count, TILE, out_weight.shape[1]), jnp.bfloat16),
            pltpu.VMEM((9, chans, TILE), jnp.float32),
            pltpu.VMEM((2, blocks, 8, TILE), jnp.float32),
            dma((6,)),
            dma((2,)),
            dma((2,)),
        ]
        + [dma((2, planes, CUTS))] * 4
        + [dma((2, 2, planes, CUTS))] * 2
        + [dma((count,))] * 8
        + [dma((2, planes))] * 4
        + [dma((2, 2, planes))] * 2
        + [dma((PARTS + 1, count))] * 2
        + [dma((2, planes, 2))] * 2,
        compiler_params=pltpu.CompilerParams(
            collective_id=0, has_side_effects=True, vmem_limit_bytes=61 * 1024 * 1024
        ),
    )(in_weight.transpose(1, 0, 2), filters, tokens, out_weight, short_taps, doc_lengths)


def fits(tokens, in_weight, filters, out_weight):
    count = lax.axis_size("ctx")
    rows, model = tokens.shape
    return (
        count % 2 == 0
        and count >= 6
        and lax.axis_size("chan") == 2
        and lax.axis_size("groups") == 2
        and in_weight.shape[0] == 2 * TILE
        and in_weight.shape[2] == count * TILE
        and filters.shape[1] == 2 * TILE
        and rows == 2 * TILE
        and out_weight.shape[1] == 2 * TILE
        and model == 2 * TILE * count
        and count * rows * model * 2 <= 8 * 1024 * 1024
    )


def layer(tokens, in_weight, short_taps, filters, doc_lengths, out_weight):
    if fits(tokens, in_weight, filters, out_weight):
        return fused(tokens, in_weight, short_taps, filters, doc_lengths, out_weight)
    return shards(tokens, in_weight, short_taps, filters, doc_lengths, out_weight)


def solution(mesh):
    placed = (
        P(("groups", "ctx"), None),
        P("ctx", None, "chan"),
        P(None, None, "chan"),
        P("chan", "ctx"),
        P("groups"),
        P("chan", "ctx"),
    )
    return jax.shard_map(
        layer,
        mesh=mesh,
        in_specs=placed,
        out_specs=P(("groups", "ctx", "chan"), None),
        check_vma=False,
    )
```

```python
import functools
import math

import jax
import jax.numpy as jnp
from jax import lax
from jax.experimental import pallas as pl
from jax.experimental.pallas import tpu as pltpu
from jax.sharding import PartitionSpec as P

def contract(form, left, right):
    return jnp.einsum(form, left, right, precision=lax.Precision.HIGHEST)


def angle_table(rows, cols, period):
    product = lax.broadcasted_iota(jnp.int32, (rows, cols), 0) * lax.broadcasted_iota(
        jnp.int32, (rows, cols), 1
    )
    theta = (product % period).astype(jnp.float32) * (2.0 * math.pi / period)
    return (jnp.cos(theta), jnp.sin(theta))


def document_ids(doc_lengths, seq_len):
    count = doc_lengths.shape[0]
    order = lax.broadcasted_iota(jnp.int32, (count, count), 0)
    before = order >= lax.broadcasted_iota(jnp.int32, (count, count), 1)
    ends = jnp.sum(jnp.where(before, doc_lengths[None, :], 0), axis=1)
    places = lax.broadcasted_iota(jnp.int32, (seq_len, ends.shape[0]), 0)
    return jnp.sum((places >= ends[None, :]).astype(jnp.int32), axis=1)


def short_conv(streams, taps, doc_id):
    result = taps[:, 0, :, None] * streams
    for lag in (1, 2):
        moved = jnp.pad(streams, ((0, 0), (0, 0), (lag, 0)))[:, :, :-lag]
        linked = jnp.concatenate((jnp.zeros((lag,), bool), doc_id[lag:] == doc_id[:-lag]))
        result = result + taps[:, lag, :, None] * jnp.where(linked[None, None, :], moved, 0.0)
    return result


def causal_filter(gated, kernel_rows):
    count, seq_len = gated.shape
    width = math.gcd(seq_len, 128)
    half = seq_len // width
    span = 2 * half
    total = span * width
    signal = gated.reshape(count, half, width)
    kernel = kernel_rows.reshape(count, half, width)
    cos_b, sin_b = angle_table(span, span, span)
    twist_c, twist_s = angle_table(span, width, total)
    cos_a, sin_a = angle_table(width, width, width)

    def forward(values):
        padded = jnp.concatenate((values, jnp.zeros_like(values)), 1)
        real_part = contract("kb,cba->cka", cos_b, padded)
        imag_part = -contract("kb,cba->cka", sin_b, padded)
        turned_r = real_part * twist_c + imag_part * twist_s
        turned_i = imag_part * twist_c - real_part * twist_s
        spec_r = contract("cka,aj->ckj", turned_r, cos_a) + contract("cka,aj->ckj", turned_i, sin_a)
        spec_i = contract("cka,aj->ckj", turned_i, cos_a) - contract("cka,aj->ckj", turned_r, sin_a)
        return (spec_r, spec_i)

    sig_r, sig_i = forward(signal)
    ker_r, ker_i = forward(kernel)
    prod_r = sig_r * ker_r - sig_i * ker_i
    prod_i = sig_r * ker_i + sig_i * ker_r
    back_r = contract("ckj,aj->cka", prod_r, cos_a) - contract("ckj,aj->cka", prod_i, sin_a)
    back_i = contract("ckj,aj->cka", prod_i, cos_a) + contract("ckj,aj->cka", prod_r, sin_a)
    untwist_r = back_r * twist_c - back_i * twist_s
    untwist_i = back_i * twist_c + back_r * twist_s
    blocks = contract("bk,cka->cba", cos_b, untwist_r) - contract("bk,cka->cba", sin_b, untwist_i)
    blocks = blocks[:, :half]
    return (blocks / total).reshape(count, seq_len)


def shards(tokens, in_weight, short_taps, filters, doc_lengths, out_weight):
    width_dev = in_weight.shape[2]
    group_width = width_dev // lax.axis_size("ctx")
    streams = jnp.einsum(
        "dsc,td->sct",
        lax.all_gather(in_weight, "ctx", axis=0, tiled=True),
        tokens,
        preferred_element_type=jnp.float32,
    )
    packed = jnp.concatenate((streams.astype(jnp.bfloat16), filters[None]), 0)
    spread = lax.all_to_all(packed, "ctx", split_axis=1, concat_axis=2, tiled=True)
    taps = lax.dynamic_slice_in_dim(
        short_taps, lax.axis_index("ctx") * group_width, group_width, 2
    ).astype(jnp.float32)
    seq_len = spread.shape[2]
    doc_id = document_ids(doc_lengths, seq_len)
    conv = short_conv(spread[:3].astype(jnp.float32), taps, doc_id)
    filtered = causal_filter(conv[0] * conv[2], spread[3].astype(jnp.float32))
    mixed = (conv[1] * filtered).astype(jnp.bfloat16)
    returned = lax.all_to_all(mixed, "ctx", split_axis=1, concat_axis=0, tiled=True)
    partial_out = lax.dot_general(
        returned,
        lax.all_gather(out_weight, "ctx", axis=1, tiled=True),
        (((0,), (0,)), ((), ())),
        preferred_element_type=jnp.float32,
    )
    return lax.psum_scatter(partial_out, "chan", scatter_dimension=0, tiled=True).astype(
        jnp.bfloat16
    )


TILE = 128
HALF = 64
THICK = 16
MESH = pl.DeviceIdType.MESH


def spread_taps(taps_ref, taps, chans, me):
    for s in range(3):
        rows = taps_ref[s, :, pl.ds(pl.multiple_of(me * chans, TILE), chans)].astype(jnp.float32)
        for lag in range(3):
            taps[3 * s + lag] = jnp.broadcast_to(rows[lag : lag + 1, :], (TILE, chans)).T


def mark_links(docs_ref, keep, blocks):
    lane = lax.broadcasted_iota(jnp.int32, (8, TILE), 1)
    ends = []
    for j in range(docs_ref.shape[0]):
        ends.append(docs_ref[j] + ends[-1] if j else docs_ref[j])
    for b in range(blocks):
        place = lane + b * TILE
        for lag in (1, 2):
            linked = place >= lag
            for end in ends:
                linked = jnp.logical_and(
                    linked, jnp.logical_or(place < end, place - lag >= end)
                )
            keep[lag - 1, b] = linked.astype(jnp.float32)


def build_band(index, kernels, bands):
    seq = kernels.shape[1]
    lane = lax.broadcasted_iota(jnp.int32, (THICK, TILE), 1)
    place = lane % HALF - lax.broadcasted_iota(jnp.int32, (THICK, TILE), 0)
    low = lane < HALF
    for pair in range(2):
        rows = [
            jnp.broadcast_to(kernels[pl.ds(4 * index + 2 * pair + u, 1), :], (THICK, seq))
            for u in range(2)
        ]
        for q in range(TILE // THICK):
            moved = [
                pltpu.roll(
                    rows[u],
                    (seq - HALF * (1 - u) + q * THICK) % seq,
                    1,
                    stride=1,
                    stride_axis=0,
                )
                for u in range(2)
            ]
            for m in range(seq // TILE):
                span = slice(m * TILE, (m + 1) * TILE)
                tile = jnp.where(low, moved[0][:, span], moved[1][:, span])
                if m == 0:
                    tile = jnp.where(place + HALF >= q * THICK, tile, 0.0)
                first = (m % 2) * TILE + q * THICK
                bands[
                    index, m // 2, first : first + THICK, pair * TILE : (pair + 1) * TILE
                ] = tile.astype(jnp.bfloat16)


def filter_group(index, streams, taps, keep, bands, mixed, chans):
    blocks = keep.shape[1]
    lane = lax.broadcasted_iota(jnp.int32, (8, TILE), 1)
    sub = lax.broadcasted_iota(jnp.int32, (8, TILE), 0)
    left, top = lane < HALF, sub < 4
    second = (sub & 2) > 0
    straight = ((sub & 1) == 0) != top
    products = []
    for half in range(2):
        first = pl.multiple_of(index * 16 + 8 * half, 8)
        rows = pl.ds(first, 8)
        conv = [None] * 3
        for s in range(3):
            tap = [taps[3 * s + lag, rows, :] for lag in range(3)]
            conv[s] = []
            before = [None, None]
            for b in range(blocks):
                value = streams[s, b, rows, :]
                total = tap[0] * value
                for lag in (1, 2):
                    rolled = pltpu.roll(value, lag, 1)
                    moved = rolled
                    if b:
                        moved = jnp.where(lane < lag, before[lag - 1], rolled)
                    before[lag - 1] = rolled
                    total = total + tap[lag] * (keep[lag - 1, b] * moved)
                conv[s].append(total)
        gated = [conv[0][b] * conv[2][b] for b in range(blocks)]
        turned = [pltpu.roll(gated[b], HALF, 1) for b in range(blocks)]
        late = [
            jnp.where(left, turned[b - 1] if b else 0.0, turned[b]) for b in range(blocks)
        ]
        packed = []
        for quad in range(2):
            if quad == 0:
                rows_of = [
                    jnp.where(top, gated[b], pltpu.roll(late[b], 4, 0)) for b in range(blocks)
                ]
            else:
                rows_of = [
                    jnp.where(top, pltpu.roll(gated[b], 4, 0), late[b]) for b in range(blocks)
                ]
            now = jnp.concatenate(rows_of, axis=0).astype(jnp.bfloat16)
            old = jnp.concatenate(
                [jnp.zeros_like(rows_of[0])] + rows_of[:-1], axis=0
            ).astype(jnp.bfloat16)
            packed.append(jnp.concatenate([now, old], axis=1))
        straights, swapped = [], []
        for quad in range(2):
            which = 4 * index + 2 * half + quad
            sums = [None] * blocks
            for t in range(blocks // 2):
                height = 8 * blocks - 16 * t
                part = jnp.dot(
                    packed[quad][:height], bands[which, t], preferred_element_type=jnp.float32
                )
                for b in range(2 * t, blocks):
                    piece = part[8 * (b - 2 * t) : 8 * (b - 2 * t) + 8]
                    sums[b] = piece if sums[b] is None else sums[b] + piece
            one, two = [], []
            for b in range(blocks):
                both = jnp.where(second, sums[b][:, TILE:], sums[b][:, :TILE])
                both = jnp.where(straight, both, pltpu.roll(both, HALF, 1))
                one.append(both)
                two.append(pltpu.roll(both, 4, 0))
            straights.append(one)
            swapped.append(two)
        result = []
        for b in range(blocks):
            upper = jnp.where(left, swapped[0][b], straights[0][b])
            lower = jnp.where(left, straights[1][b], swapped[1][b])
            result.append(conv[1][b] * jnp.where(top, upper, lower))
        products.append(result)
    for b in range(blocks):
        mixed[b, pl.ds(pl.multiple_of(index * 16, 16), 16), :] = jnp.concatenate(
            [products[0][b], products[1][b]], axis=0
        ).astype(jnp.bfloat16)


def exchange_kernel(
    planes,
    cuts,
    parts,
    weight_ref,
    filters_ref,
    tokens_ref,
    outw_ref,
    taps_ref,
    docs_ref,
    out_ref,
    toks,
    raw,
    wide,
    lags,
    outw,
    streams,
    kernels,
    bands,
    mixed,
    arrived,
    turned,
    own_part,
    sent_part,
    got_part,
    taps,
    keep,
    local_sem,
    own_send,
    own_recv,
    tok_z_send,
    tok_z_recv,
    tok_x_send,
    tok_x_recv,
    tok_c_send,
    tok_c_recv,
    w_send,
    w_recv,
    w_y_send,
    w_y_recv,
    f_send,
    f_recv,
    f_y_send,
    f_y_recv,
    o_z_send,
    o_z_recv,
    o_y_send,
    o_y_recv,
    o_c_send,
    o_c_recv,
    m_send,
    m_recv,
    p_send,
    p_recv,
):
    g = lax.axis_index("groups")
    k = lax.axis_index("ctx")
    x = lax.axis_index("chan")
    z, core = k // 2, k % 2
    count = 2 * planes
    blocks = 2 * count
    rows = tokens_ref.shape[0]
    lanes = rows // 2
    piece = lanes // cuts
    depth = weight_ref.shape[1]
    half_d = depth // 2
    half_o = outw_ref.shape[0] // 2
    chans = kernels.shape[0]
    other = 2 * z + 1 - core

    def at(group=g, ctx=k, chan=x):
        return (group, ctx, chan)

    def remote(src, dst, send, recv, where):
        return pltpu.make_async_remote_copy(
            src_ref=src,
            dst_ref=dst,
            send_sem=send,
            recv_sem=recv,
            device_id=where,
            device_id_type=MESH,
        )

    def tile_of(index):
        return pl.ds(pl.multiple_of(index * TILE, TILE), TILE)

    def when(condition, action):
        pl.when(condition)(action)

    barrier = pltpu.get_barrier_semaphore()
    for step in range(1, count):
        pl.semaphore_signal(
            barrier, inc=1, device_id=at(ctx=(k + step) % count), device_id_type=MESH
        )
    pl.semaphore_signal(barrier, inc=1, device_id=at(chan=1 - x), device_id_type=MESH)
    pl.semaphore_signal(barrier, inc=1, device_id=at(group=1 - g), device_id_type=MESH)
    pl.semaphore_wait(barrier, count + 1)

    def lag_column(owner, half):
        return lags.at[:, tile_of(2 * owner + half)]

    def lags_of(owner, half):
        return filters_ref.at[tile_of(owner), tile_of(half)]

    def weight_rows(owner, half):
        return raw.at[:, pl.ds(pl.multiple_of(owner * depth + half * half_d, TILE), half_d), :]

    def weight_of(owner, half):
        return weight_ref.at[:, pl.ds(pl.multiple_of(half * half_d, TILE), half_d), tile_of(owner)]

    def tok(owner, half, cut):
        return toks.at[owner, pl.ds(pl.multiple_of(half * lanes + cut * piece, piece), piece), :]

    def outw_at(owner, half):
        return outw.at[owner, pl.ds(pl.multiple_of(half * half_o, half_o), half_o), :]

    flights = []

    def launch(copy):
        copy.start()
        flights.append(copy)
        return copy

    f_copies = [
        launch(
            remote(
                lags_of((k + step) % count, g),
                lag_column(k, g),
                f_send.at[step],
                f_recv.at[step],
                at(ctx=(k + step) % count),
            )
        )
        for step in range(1, count)
    ]

    locals_ = [
        pltpu.make_async_copy(lags_of(k, 0), lag_column(k, 0), local_sem.at[0]),
        pltpu.make_async_copy(lags_of(k, 1), lag_column(k, 1), local_sem.at[1]),
        pltpu.make_async_copy(weight_of(k, 0), weight_rows(k, 0), local_sem.at[2]),
        pltpu.make_async_copy(weight_of(k, 1), weight_rows(k, 1), local_sem.at[3]),
        pltpu.make_async_copy(tokens_ref, toks.at[k], local_sem.at[4]),
        pltpu.make_async_copy(outw_ref, outw.at[k], local_sem.at[5]),
    ]
    for copy in locals_[:2]:
        copy.start()

    guarded = []

    def present(side, step):
        return z >= step if side == 0 else z + step < planes

    def onward(side):
        return z + 1 < planes if side == 0 else z >= 1

    def origin(side, step):
        return 2 * (z - step if side == 0 else z + step) + core

    def beyond(side):
        return at(ctx=2 * (z + 1 if side == 0 else z - 1) + core)

    def hop(side, step, make, only=None):
        ready = onward(side)
        if only is not None:
            ready = jnp.logical_and(ready, only)
        if step > 1:
            ready = jnp.logical_and(ready, present(side, step - 1))

        def go():
            make().start()

        when(ready, go)
        guarded.append((ready, make))

    def tok_hop(side, step, cut):
        def make():
            if step == 1:
                source = tokens_ref.at[
                    pl.ds(pl.multiple_of(x * lanes + cut * piece, piece), piece), :
                ]
            else:
                source = tok(origin(side, step - 1), x, cut)
            return remote(
                source,
                tok(origin(side, step - 1), x, cut),
                tok_z_send.at[side, step, cut],
                tok_z_recv.at[side, step, cut],
                beyond(side),
            )

        hop(side, step, make)

    for cut in range(cuts):
        for side in range(2):
            tok_hop(side, 1, cut)

    w_copies = [
        launch(
            remote(
                weight_of((k + step) % count, g),
                weight_rows(k, g),
                w_send.at[step],
                w_recv.at[step],
                at(ctx=(k + step) % count),
            )
        )
        for step in range(1, count)
    ]
    for copy in locals_[2:]:
        copy.start()
    core_own = launch(
        remote(tokens_ref, toks.at[k], own_send.at[0], own_recv.at[0], at(ctx=other))
    )
    core_own_o = launch(
        remote(outw_ref, outw.at[k], own_send.at[1], own_recv.at[1], at(ctx=other))
    )

    spread_taps(taps_ref, taps, chans, k)
    mark_links(docs_ref, keep, blocks)

    fy_copies = []
    for step in range(1, count):
        f_copies[step - 1].wait_recv()
        came = lag_column((k + count - step) % count, g)
        fy_copies.append(
            launch(remote(came, came, f_y_send.at[step], f_y_recv.at[step], at(group=1 - g)))
        )
    for copy in fy_copies:
        copy.wait_recv()
    for copy in locals_[:2]:
        copy.wait()
    kernels[...] = lags[...].astype(jnp.float32)

    total = bands.shape[0]
    done = [0]

    def work(amount):
        first, last = done[0], min(done[0] + amount, total)
        done[0] = last

        def body(index, carry):
            build_band(index, kernels, bands)
            return carry

        if last > first:
            lax.fori_loop(first, last, body, 0)

    def tok_z(side, step, cut):
        came = tok(origin(side, step), x, cut)
        return remote(
            came, came, tok_z_send.at[side, step, cut], tok_z_recv.at[side, step, cut], at(ctx=other)
        )

    def tok_x(side, step, half, cut):
        came = tok(origin(side, step), half, cut)
        return remote(
            came, came, tok_x_send.at[side, step, cut], tok_x_recv.at[side, step, cut], at(chan=1 - x)
        )

    def tok_c(side, step, half, which, cut):
        came = tok(origin(side, step), half, cut)
        return remote(
            came,
            came,
            tok_c_send.at[which, side, step, cut],
            tok_c_recv.at[which, side, step, cut],
            at(ctx=other),
        )

    def tok_relay(step, cut):
        for side in range(2):

            def arrive(side=side):
                tok_z(side, step, cut).wait_recv()

            when(present(side, step), arrive)
            if step + 1 < planes:
                tok_hop(side, step + 1, cut)

            def share(side=side):
                tok_x(side, step, x, cut).start()
                tok_c(side, step, x, 0, cut).start()

            when(present(side, step), share)

    def tok_cross(step, cut):
        for side in range(2):

            def arrive(side=side):
                tok_x(side, step, 1 - x, cut).wait_recv()
                tok_c(side, step, 1 - x, 1, cut).start()

            when(present(side, step), arrive)

    def project(index, carry):
        value = lax.dot_general(
            wide[...],
            toks[index],
            (((1,), (1,)), ((), ())),
            preferred_element_type=jnp.float32,
        )
        value = value.astype(jnp.bfloat16).astype(jnp.float32)
        for s in range(3):
            for h in range(2):
                streams[s, 2 * index + h] = value[
                    s * chans : (s + 1) * chans, h * TILE : (h + 1) * TILE
                ]
        return carry

    def tok_done(step):
        for side in range(2):

            def arrive(side=side):
                for cut in range(cuts):
                    for which in range(2):
                        tok_c(side, step, which, which, cut).wait_recv()

                def both(index, carry):
                    return project(2 * (origin(side, step) // 2) + index, carry)

                lax.fori_loop(0, 2, both, 0)

            when(present(side, step), arrive)

    def outw_hop(side, step, only=None):
        def make():
            if step == 1:
                source = outw_ref.at[pl.ds(pl.multiple_of(g * half_o, half_o), half_o), :]
            else:
                source = outw_at(origin(side, step - 1), g)
            return remote(
                source,
                outw_at(origin(side, step - 1), g),
                o_z_send.at[side, step],
                o_z_recv.at[side, step],
                beyond(side),
            )

        hop(side, step, make, only)

    def outw_move(kind, side, step, half):
        came = outw_at(origin(side, step), half)
        if kind == "z":
            sems, where = (o_z_send.at[side, step], o_z_recv.at[side, step]), at(ctx=other)
        elif kind == "y":
            sems, where = (o_y_send.at[side, step], o_y_recv.at[side, step]), at(group=1 - g)
        else:
            which = int(kind)
            sems = (o_c_send.at[which, side, step], o_c_recv.at[which, side, step])
            where = at(ctx=other)
        return remote(came, came, sems[0], sems[1], where)

    middle = jnp.logical_and(z >= 1, z + 1 < planes)

    def outw_relay(step, who):
        for side in range(2):
            here = jnp.logical_and(present(side, step), who)

            def arrive(side=side):
                outw_move("z", side, step, g).wait_recv()

            when(here, arrive)
            if step + 1 < planes:
                outw_hop(side, step + 1, who)

            def share(side=side):
                outw_move("y", side, step, g).start()
                outw_move("0", side, step, g).start()

            when(here, share)

    def outw_last(step):
        for side in range(2):

            def arrive(side=side):
                outw_move("y", side, step, 1 - g).wait_recv()
                outw_move("1", side, step, 1 - g).start()

            when(present(side, step), arrive)

    last = planes - 1
    work(total // 4)
    for cut in range(cuts):
        tok_relay(1, cut)
        work(total // 4 // cuts)
    wy_copies = []
    for step in range(1, count):
        w_copies[step - 1].wait_recv()
        came = weight_rows((k + count - step) % count, g)
        wy_copies.append(
            launch(remote(came, came, w_y_send.at[step], w_y_recv.at[step], at(group=1 - g)))
        )
        work(1)
    for step in range(2, planes):
        for cut in range(cuts):
            if step == planes - 1:
                break
            tok_relay(step, cut)
            tok_cross(step - 1, cut)
            work(2)
    work(total)
    for copy in locals_[2:]:
        copy.wait()
    for copy in wy_copies:
        copy.wait_recv()

    def stand(index, carry):
        place = pl.ds(pl.multiple_of(index * TILE, TILE), TILE)
        for s in range(3):
            wide[s * chans : (s + 1) * chans, place] = (
                raw[s, place, :].astype(jnp.float32).T.astype(jnp.bfloat16)
            )
        return carry

    lax.fori_loop(0, raw.shape[1] // TILE, stand, 0)
    core_own.wait_recv()

    def ends(side):
        return z + 2 == planes if side == 0 else z == 1

    for side in range(2):
        outw_hop(side, 1, jnp.logical_not(ends(side)))
    for cut in range(cuts):
        tok_relay(last, cut)
        if last > 1:
            tok_cross(last - 1, cut)
        if cut == 0:
            project(k, 0)
            project(other, 0)
        elif cut == 1:
            for step in range(1, last - 1):
                tok_done(step)
    for side in range(2):
        outw_hop(side, 1, ends(side))
    outer = jnp.logical_not(middle)
    outw_relay(1, middle)
    tok_done(last - 1)
    for cut in range(cuts):
        tok_cross(last, cut)
    for step in range(2, last):
        outw_relay(step, middle)
    tok_done(last)
    outw_relay(1, outer)

    groups = chans // 16 // parts

    def filter_step(index, carry):
        filter_group(index, streams, taps, keep, bands, mixed, chans)
        return carry

    m_copies = []
    for part in range(parts):
        lax.fori_loop(part * groups, (part + 1) * groups, filter_step, 0)
        span = pl.ds(part * groups * 16, groups * 16)
        for step in range(1, count):
            to = (k + step) % count
            m_copies.append(
                launch(
                    remote(
                        mixed.at[2 * to + 1 - x, span, :],
                        arrived.at[k, 1 - x, span, :],
                        m_send.at[part, step],
                        m_recv.at[part, step],
                        at(ctx=to),
                    )
                )
            )
        if part == parts // 2 - 1:
            for step in range(2, last):
                outw_relay(step, outer)
        if part == parts // 2:
            outw_last(1)
    own_mixed = pltpu.make_async_copy(
        mixed.at[pl.ds(2 * k, 2)], arrived.at[k], local_sem.at[0]
    )
    own_mixed.start()
    late_copies = [
        launch(
            remote(
                mixed.at[2 * ((k + step) % count) + x],
                arrived.at[k, x],
                m_send.at[parts, step],
                m_recv.at[parts, step],
                at(ctx=(k + step) % count),
            )
        )
        for step in range(1, count)
    ]
    own_mixed.wait()

    def stand_rows(h):
        for owner in range(count):
            turned[h, :, owner * chans : (owner + 1) * chans] = (
                arrived[owner, h].astype(jnp.float32).T.astype(jnp.bfloat16)
            )

    for copy in m_copies:
        copy.wait_recv()
    stand_rows(1 - x)

    wide_e = outw_ref.shape[1]

    def give(owner, side, step, side_core):
        copy = remote(
            sent_part.at[owner],
            got_part.at[owner],
            p_send.at[side, step, side_core],
            p_recv.at[side, step, side_core],
            at(chan=1 - x),
        )
        return copy

    def multiply(owner):
        sent_part[owner] = jnp.dot(
            turned[1 - x], outw[owner], preferred_element_type=jnp.float32
        ).astype(jnp.bfloat16)

    def keep_own(owner):
        own_part[owner] = jnp.dot(
            turned[x], outw[owner], preferred_element_type=jnp.float32
        )

    def finish(owner):
        span = pl.ds(pl.multiple_of(owner * wide_e, TILE), wide_e)
        out_ref[:, span] = (own_part[owner] + got_part[owner].astype(jnp.float32)).astype(
            jnp.bfloat16
        )

    def pair_of(side, step):
        return [2 * (origin(side, step) // 2) + c for c in range(2)]

    def each(step, action):
        for side in range(2):
            if step == 0:
                if side == 0:
                    action(side, step)
                continue

            def go(side=side):
                action(side, step)

            when(present(side, step), go)

    def send_part(side, step):
        for kind in range(2):
            if step:
                half = g if kind == 0 else 1 - g
                outw_move(str(kind), side, step, half).wait_recv()
        for c, owner in enumerate(pair_of(side, step)):
            multiply(owner)
            give(owner, side, step, c).start()

    def own_dots(side, step):
        for owner in pair_of(side, step):
            keep_own(owner)

    def take_part(side, step):
        for c, owner in enumerate(pair_of(side, step)):
            give(owner, side, step, c).wait_recv()
            finish(owner)

    def part_gone(side, step):
        for c, owner in enumerate(pair_of(side, step)):
            give(owner, side, step, c).wait_send()

    core_own_o.wait_recv()
    for step in range(2):
        each(step, send_part)
    outw_relay(last, outer)
    for step in range(2, last):
        outw_last(step)
        each(step, send_part)
    for copy in late_copies:
        copy.wait_recv()
    stand_rows(x)
    for step in range(last):
        each(step, own_dots)
    outw_last(last)
    each(last, send_part)
    each(last, own_dots)
    for step in range(planes):
        each(step, take_part)
    for step in range(planes):
        each(step, part_gone)

    for copy in flights:
        copy.wait_send()
    for ready, make in guarded:

        def left(make=make):
            make().wait_send()

        when(ready, left)
    for step in range(1, planes):
        for side in range(2):

            def gone(side=side, step=step):
                for cut in range(cuts):
                    tok_x(side, step, x, cut).wait_send()
                    tok_c(side, step, x, 0, cut).wait_send()
                    tok_c(side, step, 1 - x, 1, cut).wait_send()
                outw_move("y", side, step, g).wait_send()
                outw_move("0", side, step, g).wait_send()
                outw_move("1", side, step, 1 - g).wait_send()

            when(present(side, step), gone)


CUTS = 4
PARTS = 8


def fused(tokens, in_weight, short_taps, filters, doc_lengths, out_weight):
    count = lax.axis_size("ctx")
    chans = in_weight.shape[2] // count
    rows, model = tokens.shape
    seq_len = filters.shape[1] * count
    blocks = seq_len // TILE
    planes = count // 2
    dma = pltpu.SemaphoreType.DMA
    anywhere = pl.BlockSpec(memory_space=pl.ANY)
    vmem = pl.BlockSpec(memory_space=pltpu.VMEM)
    return pl.pallas_call(
        functools.partial(exchange_kernel, planes, CUTS, PARTS),
        out_shape=jax.ShapeDtypeStruct((rows // 2, model), jnp.bfloat16),
        in_specs=[anywhere] * 4 + [vmem, pl.BlockSpec(memory_space=pltpu.SMEM)],
        out_specs=vmem,
        scratch_shapes=[
            pltpu.VMEM((count, rows, model), jnp.bfloat16),
            pltpu.VMEM((3, model, chans), jnp.bfloat16),
            pltpu.VMEM((3 * chans, model), jnp.bfloat16),
            pltpu.VMEM((chans, seq_len), jnp.bfloat16),
            pltpu.VMEM((count,) + out_weight.shape, jnp.bfloat16),
            pltpu.VMEM((3, blocks, chans, TILE), jnp.float32),
            pltpu.VMEM((chans, seq_len), jnp.float32),
            pltpu.VMEM((chans // 4, blocks // 2, 2 * TILE, 2 * TILE), jnp.bfloat16),
            pltpu.VMEM((blocks, chans, TILE), jnp.bfloat16),
            pltpu.VMEM((count, 2, chans, TILE), jnp.bfloat16),
            pltpu.VMEM((2, TILE, count * chans), jnp.bfloat16),
            pltpu.VMEM((count, TILE, out_weight.shape[1]), jnp.float32),
            pltpu.VMEM((count, TILE, out_weight.shape[1]), jnp.bfloat16),
            pltpu.VMEM((count, TILE, out_weight.shape[1]), jnp.bfloat16),
            pltpu.VMEM((9, chans, TILE), jnp.float32),
            pltpu.VMEM((2, blocks, 8, TILE), jnp.float32),
            dma((6,)),
            dma((2,)),
            dma((2,)),
        ]
        + [dma((2, planes, CUTS))] * 4
        + [dma((2, 2, planes, CUTS))] * 2
        + [dma((count,))] * 8
        + [dma((2, planes))] * 4
        + [dma((2, 2, planes))] * 2
        + [dma((PARTS + 1, count))] * 2
        + [dma((2, planes, 2))] * 2,
        compiler_params=pltpu.CompilerParams(
            collective_id=0, has_side_effects=True, vmem_limit_bytes=61 * 1024 * 1024
        ),
    )(in_weight.transpose(1, 0, 2), filters, tokens, out_weight, short_taps, doc_lengths)


def fits(tokens, in_weight, filters, out_weight):
    count = lax.axis_size("ctx")
    rows, model = tokens.shape
    return (
        count % 2 == 0
        and count >= 6
        and lax.axis_size("chan") == 2
        and lax.axis_size("groups") == 2
        and in_weight.shape[0] == 2 * TILE
        and in_weight.shape[2] == count * TILE
        and filters.shape[1] == 2 * TILE
        and rows == 2 * TILE
        and out_weight.shape[1] == 2 * TILE
        and model == 2 * TILE * count
        and count * rows * model * 2 <= 8 * 1024 * 1024
    )


def layer(tokens, in_weight, short_taps, filters, doc_lengths, out_weight):
    if fits(tokens, in_weight, filters, out_weight):
        return fused(tokens, in_weight, short_taps, filters, doc_lengths, out_weight)
    return shards(tokens, in_weight, short_taps, filters, doc_lengths, out_weight)


def solution(mesh):
    placed = (
        P(("groups", "ctx"), None),
        P("ctx", None, "chan"),
        P(None, None, "chan"),
        P("chan", "ctx"),
        P("groups"),
        P("chan", "ctx"),
    )
    return jax.shard_map(
        layer,
        mesh=mesh,
        in_specs=placed,
        out_specs=P(("groups", "ctx", "chan"), None),
        check_vma=False,
    )
```
